512 devices in a mesh: off: 2 (over x_hi), il: 8 (over y), xl: 32 (over x_lo, z, core).
Axes of the slice: x: 4 (x_hi: 2, x_lo: 2; x = x_hi * 2 + x_lo), y: 8, z: 8, core: 2. Of those that a mesh axis runs over, the one named last changes fastest.
Arguments:
- data: float32 [32, 128, 16, 1024], P('il', 'xl', 'off'), may hold values from -6 to 6
- offset_weight: float32 [16], P('off'), may hold values from 0.2 to 5
Outputs:
- slope: float32 [32, 128, 16, 1024], P('il', 'xl', 'off')
- stacked: float32 [32, 128, 1024], P('il', 'xl')
The draws below stay inside these ranges and needn't reach their ends.
All inputs are finite; a program needn't handle non-finite values.
Results may differ from the reference program's by a relative error of at most 0.0003.
Values sent between devices are 32-bit elements; how exact they have to be, the bound alone decides.
A program may use at most 64 MiB of HBM per device.

```python
import math
import jax
import jax.numpy as jnp
from jax import lax

NT = 1024
ITERS = 3
NIL = 32
NXL = 128
NOFF = 16


def level_of(own_key, dims, pieces, low, high):
    loudness = 1.0
    for position, shards_of in pieces:
        heights = jax.random.uniform(jax.random.fold_in(jax.random.fold_in(own_key, 6), position), (shards_of,), jnp.float32, low / len(pieces), high / len(pieces))
        loudness = loudness * jnp.repeat(jnp.exp(heights), dims[position] // shards_of).reshape((-1,) + (1,) * (len(dims) - 1 - position))
    return loudness


def normal_values(stream_key, shape, spread, limit, split=(), kind=jnp.bfloat16):
    result = jax.random.normal(stream_key, shape, jnp.float32) * spread
    if len(split) > 0:
        result = level_of(stream_key, shape, split, -0.22, 0.18) * result
    return jnp.clip(result, min=-limit, max=limit).astype(kind)


def setup_inputs(seed: int = 0) -> dict:
    key_list = jax.random.split(jax.random.key(seed), 3)
    return {
        "data": normal_values(key_list[0], (NIL, NXL, NOFF, NT), 1.0, 6.0, ((0, 8), (1, 32), (2, 2)), jnp.float32),
        "offset_weight": jnp.clip(jnp.exp(math.log(5.0) - 3.218876 * jax.random.uniform(key_list[1], (NOFF,), jnp.float32) ** level_of(key_list[1], (NOFF,), ((0, 2),), -0.2, 0.2)), 0.2, 5.0),
    }


damping = 0.05

def weighted_box(padded, axis):
    length = padded.shape[axis] - 2
    left = lax.slice_in_dim(padded, 0, length, axis=axis)
    middle = lax.slice_in_dim(padded, 1, length + 1, axis=axis)
    right = lax.slice_in_dim(padded, 2, length + 2, axis=axis)
    return 0.25 * left + 0.5 * middle + 0.25 * right

def padded_along(field, axis):
    widths = [(0, 0)] * field.ndim
    widths[axis] = (1, 1)
    return jnp.pad(field, widths)

def smooth(field):
    for axis in (3, 0, 1, 2):
        field = weighted_box(padded_along(field, axis), axis)
    return field

def time_derivative(field):
    padded = padded_along(field, 3)
    return 0.5 * (padded[..., 2:] - padded[..., :-2])

def reference(data, offset_weight):
    following = jnp.concatenate([data[:, :, 1:, :], jnp.zeros_like(data[:, :, :1, :])], axis=2)
    residual = following - data
    gradient = 0.5 * (time_derivative(data) + time_derivative(following))
    denominator = smooth(gradient * gradient) + damping
    slope = jnp.zeros_like(data)
    for step in range(ITERS):
        slope = slope - smooth(gradient * (residual + slope * gradient)) / denominator
    times = jnp.arange(NT, dtype=jnp.float32) + 1.0
    offsets = jnp.arange(NOFF, dtype=jnp.float32) + 0.5
    squared = times * times - times * offsets[:, None] * slope
    target = jnp.sqrt(jnp.maximum(squared, 1.0)) - 1.0

    def push_row(item):
        traces, places = item
        count = traces.shape[0] * traces.shape[1]
        traces = traces.reshape(count, NT)
        places = places.reshape(count, NT)
        lower = jnp.floor(places)
        upper_weight = places - lower
        index = jnp.minimum(lower, float(NT)).astype(jnp.int32)
        base = (jnp.arange(count, dtype=jnp.int32) * (NT + 2))[:, None]
        segments = count * (NT + 2)
        moved = jax.ops.segment_sum(((1.0 - upper_weight) * traces).reshape(-1), (base + index).reshape(-1), num_segments=segments)
        moved = moved + jax.ops.segment_sum((upper_weight * traces).reshape(-1), (base + index + 1).reshape(-1), num_segments=segments)
        return moved.reshape(count, NT + 2)[:, :NT]
    corrected = lax.map(push_row, (data, target)).reshape(data.shape)
    weighted = lax.optimization_barrier(jnp.sum(corrected * offset_weight[None, None, :, None], axis=2))
    return (slope, weighted / jnp.sum(offset_weight))
```

```python
import jax
import jax.numpy as jnp
from jax import lax
from jax.experimental import pallas as pl
from jax.experimental.pallas import tpu as pltpu
from jax.sharding import PartitionSpec as P

ITERS = 3


damping = 0.05


def extended(block, sides, width):
    for axis, dim in sides:
        count = lax.axis_size(axis)
        forward = [(i, i + 1) for i in range(count - 1)]
        backward = [(target, source) for source, target in forward]
        low = lax.ppermute(
            lax.slice_in_dim(block, block.shape[dim] - width, None, axis=dim), axis, forward
        )
        high = lax.ppermute(lax.slice_in_dim(block, 0, width, axis=dim), axis, backward)
        block = jnp.concatenate([low, block, high], axis=dim)
    return block


def passed_along(x, axis, by):
    devices = lax.axis_size(axis)
    pairs = [(i, i + by) for i in range(devices) if 0 <= i + by < devices]
    return lax.ppermute(x, axis, pairs)


def weighted_box(padded, axis):
    length = padded.shape[axis] - 2
    left = lax.slice_in_dim(padded, 0, length, axis=axis)
    middle = lax.slice_in_dim(padded, 1, length + 1, axis=axis)
    right = lax.slice_in_dim(padded, 2, length + 2, axis=axis)
    return 0.25 * left + 0.5 * middle + 0.25 * right


def padded_along(field, axis):
    widths = [(0, 0)] * field.ndim
    widths[axis] = (1, 1)
    return jnp.pad(field, widths)


def smooth(field):
    field = weighted_box(padded_along(field, 3), 3)
    padded = extended(field, (("off", 2), ("il", 0), ("xl", 1)), 1)
    padded = weighted_box(padded, 0)
    padded = weighted_box(padded, 1)
    return weighted_box(padded, 2)


def time_derivative(field):
    padded = padded_along(field, 3)
    return 0.5 * (padded[..., 2:] - padded[..., :-2])


T = 1024
NA = 16
NB = 64
KC = 512


def moveout_kernel(first_ref, w_ref, data_ref, slope_ref, out_ref):
    tt = lax.broadcasted_iota(jnp.int32, (8, T), 1).astype(jnp.float32) + 1.0
    hh = lax.broadcasted_iota(jnp.int32, (8, T), 0).astype(jnp.float32) + (0.5 + first_ref[0])
    tth = tt * hh
    ttq = tt * tt
    w = w_ref[...]
    rows = lax.broadcasted_iota(jnp.int32, (NA, 128), 0)
    rows = jnp.where(rows < 8, 2 * rows, 2 * rows - 15)
    ia = rows.astype(jnp.float32).astype(jnp.bfloat16)
    ib = lax.broadcasted_iota(jnp.int32, (NB, 128), 0).astype(jnp.float32).astype(jnp.bfloat16)
    zero = jnp.zeros((NA, 128), jnp.bfloat16)
    one_b = jnp.ones((NB, 128), jnp.bfloat16)
    zero_b = jnp.zeros((NB, 128), jnp.bfloat16)
    lane = lax.broadcasted_iota(jnp.int32, (8, 128), 1)
    row = lax.broadcasted_iota(jnp.int32, (8, 128), 0)

    def midpoint(m, carry):
        s = slope_ref[m]
        place = jnp.sqrt(jnp.maximum(ttq - tth * s, 1.0)) - 1.0
        low = jnp.floor(place)
        f = place - low
        idx = jnp.minimum(low, float(T))
        a = jnp.floor(idx * (1.0 / NB))
        b = idx - a * NB
        v = data_ref[m] * w
        x1 = v * f
        x0 = v - x1
        x0h = x0.astype(jnp.bfloat16).astype(jnp.float32)
        x1h = x1.astype(jnp.bfloat16).astype(jnp.float32)
        values = (x0h, x0 - x0h, x1h, x1 - x1h)
        acc = jnp.zeros((4 * NA, NB), jnp.float32)
        for h in range(8):
            for c in range(0, T, KC):
                left, right = [], []
                for l in range(c, c + KC, 128):
                    def spread(x, n):
                        part = x[h:h + 1, l:l + 128]
                        return jnp.broadcast_to(part, (n, 128)).astype(jnp.bfloat16)
                    hit = spread(a, NA) == ia
                    left.append(jnp.concatenate(
                        [jnp.where(hit, spread(x, NA), zero) for x in values], axis=0))
                    right.append(jnp.where(spread(b, NB) == ib, one_b, zero_b))
                acc = acc + lax.dot_general(
                    jnp.concatenate(left, axis=1), jnp.concatenate(right, axis=1),
                    (((1,), (1,)), ((), ())), preferred_element_type=jnp.float32)
        lower = acc[:NA] + acc[NA:2 * NA]
        upper = acc[2 * NA:3 * NA] + acc[3 * NA:]
        lower = jnp.concatenate([lower[:8], lower[8:]], axis=1)
        upper = jnp.concatenate([upper[:8], upper[8:]], axis=1)
        upper = pltpu.roll(upper, 1, 1)
        before = pltpu.roll(upper, 1, 0)
        upper = jnp.where(lane == 0, jnp.where(row == 0, 0.0, before), upper)
        out_ref[m] = lower + upper
        return carry

    lax.fori_loop(0, 16, midpoint, 0)


def moveout(first, w, data, slope):
    return pl.pallas_call(
        moveout_kernel,
        out_shape=jax.ShapeDtypeStruct((16, 8, 128), jnp.float32),
        in_specs=[pl.BlockSpec(memory_space=pltpu.SMEM)]
        + [pl.BlockSpec(memory_space=pltpu.VMEM)] * 3,
        out_specs=pl.BlockSpec(memory_space=pltpu.VMEM),
        name="moveout",
    )(first, w, data, slope)


def shards(data, offset_weight):
    local_offsets = data.shape[2]
    samples = data.shape[3]
    next_rows = passed_along(data[:, :, :1, :], "off", -1)
    following = jnp.concatenate([data[:, :, 1:, :], next_rows], axis=2)
    residual = following - data
    gradient = 0.5 * (time_derivative(data) + time_derivative(following))
    denominator = smooth(gradient * gradient) + damping
    slope = jnp.zeros_like(data)
    for step in range(ITERS):
        slope = slope - smooth(gradient * (residual + slope * gradient)) / denominator
    first_offset = (lax.axis_index("off") * local_offsets).astype(jnp.float32)
    partial = moveout(
        first_offset.reshape(1), offset_weight.reshape(8, 1),
        data.reshape(16, 8, T), slope.reshape(16, 8, T))
    packed = jnp.concatenate(
        [partial.reshape(4, 4, T), jnp.full((4, 4, 128), jnp.sum(offset_weight))], axis=2)
    total = packed + lax.ppermute(packed, "off", [(0, 1), (1, 0)])
    stacked = total[:, :, :T] / total[:, :, T:T + 1]
    return (slope, stacked)


def solution(mesh):
    return jax.shard_map(
        shards,
        mesh=mesh,
        in_specs=(P("il", "xl", "off", None), P("off")),
        out_specs=(P("il", "xl", "off", None), P("il", "xl", None)),
        check_vma=False,
    )
```

```python
import jax
import jax.numpy as jnp
from jax import lax
from jax.experimental import pallas as pl
from jax.experimental.pallas import tpu as pltpu
from jax.sharding import PartitionSpec as P

T = 1024
ITERS = 3
damping = 0.05
MESH = pl.DeviceIdType.MESH
STEPS = [(di, dj) for di in (-1, 0, 1) for dj in (-1, 0, 1)]
SOURCE = {-1: slice(0, 1), 0: slice(0, 4), 1: slice(3, 4)}
INNER = {-1: slice(1, 2), 0: slice(1, 5), 1: slice(4, 5)}
TARGET = {-1: slice(5, 6), 0: slice(1, 5), 1: slice(0, 1)}


def earlier(x, axis):
    n = x.shape[axis]
    at = lax.broadcasted_iota(jnp.int32, x.shape, axis)
    return jnp.where(at == 0, 0.0, pltpu.roll(x, 1, axis))


def later(x, axis):
    n = x.shape[axis]
    at = lax.broadcasted_iota(jnp.int32, x.shape, axis)
    return jnp.where(at == n - 1, 0.0, pltpu.roll(x, n - 1, axis))


def slope_kernel(counts, data_ref, out_ref, dx, d0, d1, p0, p1, gg, gr, hgg, hgr, grad, res,
                 rden, ub, uc, q2x, q2o, q3x, q3o, pq, load_sem, send_sems, recv_sems):
    n_il, n_xl = counts
    off, il, xl = lax.axis_index("off"), lax.axis_index("il"), lax.axis_index("xl")
    first = off == 0

    def exists(di, dj):
        i, j = il + di, xl + dj
        return (i >= 0) & (i < n_il) & (j >= 0) & (j < n_xl)

    def transfers(turn, field, planes):
        made = []
        for k, (di, dj) in enumerate(STEPS):
            kinds = []
            if (di, dj) != (0, 0):
                kinds.append((k, off, None, field.at[INNER[di], INNER[dj]],
                              field.at[TARGET[di], TARGET[dj]]))
            for n, (source, target, sender) in enumerate(planes):
                kinds.append((9 + 9 * n + k, 1 - off, sender, source.at[SOURCE[di], SOURCE[dj]],
                              target.at[TARGET[di], TARGET[dj]]))
            for slot, to_off, sender, source, target in kinds:
                copy = pltpu.make_async_remote_copy(
                    src_ref=source, dst_ref=target,
                    send_sem=send_sems.at[turn, slot], recv_sem=recv_sems.at[turn, slot],
                    device_id={"off": to_off, "il": il + di, "xl": xl + dj},
                    device_id_type=MESH)
                sends, takes = exists(di, dj), exists(-di, -dj)
                if sender is not None:
                    sends, takes = sends & (off == sender), takes & (off == 1 - sender)
                made.append((sends, takes, copy))
        return made

    def when_all(made, which, act):
        for item in made:
            @pl.when(item[which])
            def _():
                getattr(item[2], act)()

    load = pltpu.make_async_copy(data_ref, dx.at[1:5, 1:5], load_sem)
    load.start()
    barrier = pltpu.get_barrier_semaphore()
    for di, dj in STEPS:
        for o in (0, 1):
            if (di, dj, o) != (0, 0, 0):
                @pl.when(exists(di, dj))
                def _():
                    pl.semaphore_signal(
                        barrier, inc=1, device_id_type=MESH,
                        device_id={"off": (off + o) % 2, "il": il + di, "xl": xl + dj})
    rows_near = 1 + (il > 0).astype(jnp.int32) + (il < n_il - 1).astype(jnp.int32)
    cols_near = 1 + (xl > 0).astype(jnp.int32) + (xl < n_xl - 1).astype(jnp.int32)

    full = [(dx, (d0, d1)), (q2x, (q2o,)), (q3x, (q3o,))]
    for field, planes in full:
        for di, dj in STEPS:
            if (di, dj) != (0, 0):
                @pl.when(jnp.logical_not(exists(-di, -dj)))
                def _():
                    shape = field.at[TARGET[di], TARGET[dj]].shape
                    field[TARGET[di], TARGET[dj]] = jnp.zeros(shape, jnp.float32)
                    for plane in planes:
                        shape = plane.at[TARGET[di], TARGET[dj]].shape
                        plane[TARGET[di], TARGET[dj]] = jnp.zeros(shape, jnp.float32)

    load.wait()
    for i in range(4):
        for j in range(4):
            tile = dx[1 + i, 1 + j]
            p0[i, j:j + 1] = jnp.where(first, tile[7:8], tile[0:1])
            p1[i, j:j + 1] = tile[1:2]
    pl.semaphore_wait(barrier, 2 * rows_near * cols_near - 1)

    round1 = transfers(0, dx, [(p0, d0, None), (p1, d1, 1)])
    when_all(round1, 0, "start")
    when_all(round1, 1, "wait_recv")

    @pl.when(off == 1)
    def _():
        for i in range(6):
            for j in range(6):
                d1[i, j:j + 1] = dx[i, j, 0:1]

    keep_next = jnp.where(first, 1.0, 0.0)
    keep_before = 1.0 - keep_next
    row8 = lax.broadcasted_iota(jnp.int32, (8, T), 0)

    def gradients(i, carry):
        for j in range(6):
            d = dx[i, j]
            edge = jnp.broadcast_to(d0[i, j:j + 1] * keep_next, (8, T))
            f = jnp.where(row8 == 7, edge, pltpu.roll(d, 7, 0))
            r = f - d
            s = d + f
            g = 0.25 * (later(s, 1) - earlier(s, 1))
            gg[i, j] = g * g
            gr[i, j] = g * r
            grad[i, j] = g
            res[i, j] = r
        d, f = d0[i], d1[i]
        s = d + f
        g = 0.25 * (later(s, 1) - earlier(s, 1))
        hgg[i] = g * g
        hgr[i] = g * (f - d)
        return carry

    lax.fori_loop(0, 6, gradients, 0)

    row = lax.broadcasted_iota(jnp.int32, (8, 128), 0)

    def smooth_space(field, plane, out):
        def column(c, carry):
            lanes = pl.ds(pl.multiple_of(c * 128, 128), 128)
            sums = []
            for i in range(6):
                tiles = [field[i, j, :, lanes] for j in range(6)]
                pairs = [tiles[j] + tiles[j + 1] for j in range(5)]
                sums.append([pairs[j] + pairs[j + 1] for j in range(4)])
            halo = [plane[i, :, lanes] for i in range(6)]
            for i in range(4):
                h = halo[i] + 2.0 * halo[i + 1] + halo[i + 2]
                h = pltpu.roll(h, 1, 0) + 2.0 * h + pltpu.roll(h, 7, 0)
                before = h * keep_before
                after = h * keep_next
                for j in range(4):
                    x = sums[i][j] + 2.0 * sums[i + 1][j] + sums[i + 2][j]
                    up = jnp.broadcast_to(before[j + 1:j + 2], (8, 128))
                    down = jnp.broadcast_to(after[j + 1:j + 2], (8, 128))
                    up = jnp.where(row == 0, up, pltpu.roll(x, 1, 0))
                    down = jnp.where(row == 7, down, pltpu.roll(x, 7, 0))
                    out[i, j, :, lanes] = up + 2.0 * x + down
            return carry
        lax.fori_loop(0, 8, column, 0)

    def smooth_time(u):
        return (earlier(u, 1) + 2.0 * u + later(u, 1)) * (1.0 / 256.0)

    smooth_space(gg, hgg, ub)
    smooth_space(gr, hgr, uc)

    def start_slope(i, carry):
        for j in range(4):
            inverse = 1.0 / (smooth_time(ub[i, j]) + damping)
            rden[i, j] = inverse
            slope = -smooth_time(uc[i, j]) * inverse
            out_ref[i, j] = slope
            g = grad[i + 1, j + 1]
            q = g * (res[i + 1, j + 1] + slope * g)
            q2x[i + 1, j + 1] = q
            pq[0, i, j:j + 1] = jnp.where(first, q[7:8], q[0:1])
        return carry

    lax.fori_loop(0, 4, start_slope, 0)
    round2 = transfers(1, q2x, [(pq.at[0], q2o, None)])
    when_all(round2, 0, "start")
    when_all(round2, 1, "wait_recv")
    smooth_space(q2x, q2o, ub)

    def next_slope(i, carry):
        for j in range(4):
            slope = out_ref[i, j] - smooth_time(ub[i, j]) * rden[i, j]
            out_ref[i, j] = slope
            g = grad[i + 1, j + 1]
            q = g * (res[i + 1, j + 1] + slope * g)
            q3x[i + 1, j + 1] = q
            pq[1, i, j:j + 1] = jnp.where(first, q[7:8], q[0:1])
        return carry

    lax.fori_loop(0, 4, next_slope, 0)
    round3 = transfers(2, q3x, [(pq.at[1], q3o, None)])
    when_all(round3, 0, "start")
    when_all(round3, 1, "wait_recv")
    smooth_space(q3x, q3o, ub)

    def last_slope(i, carry):
        for j in range(4):
            out_ref[i, j] = out_ref[i, j] - smooth_time(ub[i, j]) * rden[i, j]
        return carry

    lax.fori_loop(0, 4, last_slope, 0)
    for made in (round1, round2, round3):
        when_all(made, 0, "wait_send")


def estimate(data, counts):
    tiles = pltpu.VMEM((6, 6, 8, T), jnp.float32)
    plane = pltpu.VMEM((6, 8, T), jnp.float32)
    own = pltpu.VMEM((4, 4, 8, T), jnp.float32)
    rows = pltpu.VMEM((4, 8, T), jnp.float32)
    return pl.pallas_call(
        lambda *refs: slope_kernel(counts, *refs),
        out_shape=jax.ShapeDtypeStruct((4, 4, 8, T), jnp.float32),
        in_specs=[pl.BlockSpec(memory_space=pl.ANY)],
        out_specs=pl.BlockSpec(memory_space=pltpu.VMEM),
        scratch_shapes=[tiles, plane, plane, rows, rows, tiles, tiles, plane, plane, tiles, tiles,
                        own, own, own, tiles, plane, tiles, plane,
                        pltpu.VMEM((2, 4, 8, T), jnp.float32),
                        pltpu.SemaphoreType.DMA, pltpu.SemaphoreType.DMA((3, 27)),
                        pltpu.SemaphoreType.DMA((3, 27))],
        compiler_params=pltpu.CompilerParams(
            collective_id=0, has_side_effects=True, vmem_limit_bytes=48 * 2**20),
        name="slope",
    )(data)


NA = 16
NB = 64
KC = 512


def moveout_kernel(first_ref, w_ref, data_ref, slope_ref, out_ref):
    tt = lax.broadcasted_iota(jnp.int32, (8, T), 1).astype(jnp.float32) + 1.0
    hh = lax.broadcasted_iota(jnp.int32, (8, T), 0).astype(jnp.float32) + (0.5 + first_ref[0])
    tth = tt * hh
    ttq = tt * tt
    w = w_ref[...]
    rows = lax.broadcasted_iota(jnp.int32, (NA, 128), 0)
    rows = jnp.where(rows < 8, 2 * rows, 2 * rows - 15)
    ia = rows.astype(jnp.float32).astype(jnp.bfloat16)
    ib = lax.broadcasted_iota(jnp.int32, (NB, 128), 0).astype(jnp.float32).astype(jnp.bfloat16)
    zero = jnp.zeros((NA, 128), jnp.bfloat16)
    one_b = jnp.ones((NB, 128), jnp.bfloat16)
    zero_b = jnp.zeros((NB, 128), jnp.bfloat16)
    lane = lax.broadcasted_iota(jnp.int32, (8, 128), 1)
    row = lax.broadcasted_iota(jnp.int32, (8, 128), 0)

    def midpoint(m, carry):
        s = slope_ref[m]
        place = jnp.sqrt(jnp.maximum(ttq - tth * s, 1.0)) - 1.0
        low = jnp.floor(place)
        f = place - low
        idx = jnp.minimum(low, float(T))
        a = jnp.floor(idx * (1.0 / NB))
        b = idx - a * NB
        v = data_ref[m] * w
        x1 = v * f
        x0 = v - x1
        x0h = x0.astype(jnp.bfloat16).astype(jnp.float32)
        x1h = x1.astype(jnp.bfloat16).astype(jnp.float32)
        values = (x0h, x0 - x0h, x1h, x1 - x1h)
        acc = jnp.zeros((4 * NA, NB), jnp.float32)
        for h in range(8):
            for c in range(0, T, KC):
                left, right = [], []
                for l in range(c, c + KC, 128):
                    def spread(x, n):
                        part = x[h:h + 1, l:l + 128]
                        return jnp.broadcast_to(part, (n, 128)).astype(jnp.bfloat16)
                    hit = spread(a, NA) == ia
                    left.append(jnp.concatenate(
                        [jnp.where(hit, spread(x, NA), zero) for x in values], axis=0))
                    right.append(jnp.where(spread(b, NB) == ib, one_b, zero_b))
                acc = acc + lax.dot_general(
                    jnp.concatenate(left, axis=1), jnp.concatenate(right, axis=1),
                    (((1,), (1,)), ((), ())), preferred_element_type=jnp.float32)
        lower = acc[:NA] + acc[NA:2 * NA]
        upper = acc[2 * NA:3 * NA] + acc[3 * NA:]
        lower = jnp.concatenate([lower[:8], lower[8:]], axis=1)
        upper = jnp.concatenate([upper[:8], upper[8:]], axis=1)
        upper = pltpu.roll(upper, 1, 1)
        before = pltpu.roll(upper, 1, 0)
        upper = jnp.where(lane == 0, jnp.where(row == 0, 0.0, before), upper)
        out_ref[m] = lower + upper
        return carry

    lax.fori_loop(0, 16, midpoint, 0)


def moveout(first, w, data, slope):
    return pl.pallas_call(
        moveout_kernel,
        out_shape=jax.ShapeDtypeStruct((16, 8, 128), jnp.float32),
        in_specs=[pl.BlockSpec(memory_space=pltpu.SMEM)]
        + [pl.BlockSpec(memory_space=pltpu.VMEM)] * 3,
        out_specs=pl.BlockSpec(memory_space=pltpu.VMEM),
        name="moveout",
    )(first, w, data, slope)


def shards(data, offset_weight, counts):
    slope = estimate(data, counts)
    first_offset = (lax.axis_index("off") * 8).astype(jnp.float32)
    partial = moveout(
        first_offset.reshape(1), offset_weight.reshape(8, 1),
        data.reshape(16, 8, T), slope.reshape(16, 8, T))
    packed = jnp.concatenate(
        [partial.reshape(4, 4, T), jnp.full((4, 4, 128), jnp.sum(offset_weight))], axis=2)
    total = packed + lax.ppermute(packed, "off", [(0, 1), (1, 0)])
    stacked = total[:, :, :T] / total[:, :, T:T + 1]
    return (slope, stacked)


def solution(mesh):
    counts = (mesh.shape["il"], mesh.shape["xl"])
    return jax.shard_map(
        lambda data, offset_weight: shards(data, offset_weight, counts),
        mesh=mesh,
        in_specs=(P("il", "xl", "off", None), P("off")),
        out_specs=(P("il", "xl", "off", None), P("il", "xl", None)),
        check_vma=False,
    )
```

```python
import jax
import jax.numpy as jnp
from jax import lax
from jax.experimental import pallas as pl
from jax.experimental.pallas import tpu as pltpu
from jax.sharding import PartitionSpec as P

T = 1024
NA = 16
NB = 64
damping = 0.05
MESH = pl.DeviceIdType.MESH
STEPS = [(di, dj) for di in (-1, 0, 1) for dj in (-1, 0, 1)]
SOURCE = {-1: slice(0, 1), 0: slice(0, 4), 1: slice(3, 4)}
INNER = {-1: slice(1, 2), 0: slice(1, 5), 1: slice(4, 5)}
TARGET = {-1: slice(5, 6), 0: slice(1, 5), 1: slice(0, 1)}


def earlier(x, axis):
    n = x.shape[axis]
    at = lax.broadcasted_iota(jnp.int32, x.shape, axis)
    return jnp.where(at == 0, 0.0, pltpu.roll(x, 1, axis))


def later(x, axis):
    n = x.shape[axis]
    at = lax.broadcasted_iota(jnp.int32, x.shape, axis)
    return jnp.where(at == n - 1, 0.0, pltpu.roll(x, n - 1, axis))


def moveout_kernel(counts, weight_hbm, data_ref, out_ref, stack_ref, dx, d0, d1, p0, p1, gg, gr,
                   hgg, hgr, grad, res, rden, ub, uc, q2x, q2o, q3x, q3o, pq, wsum, raw, part,
                   load_sem, send_sems, recv_sems, sum_sems, part_sems, weight_ref,
                   weight_sem, slopes, slope_sems):
    n_il, n_xl = counts
    off, il, xl = lax.axis_index("off"), lax.axis_index("il"), lax.axis_index("xl")
    first = off == 0

    def exists(di, dj):
        i, j = il + di, xl + dj
        return (i >= 0) & (i < n_il) & (j >= 0) & (j < n_xl)

    def transfers(turn, field, planes):
        made = []
        for k, (di, dj) in enumerate(STEPS):
            kinds = []
            if (di, dj) != (0, 0):
                kinds.append((k, off, None, field.at[INNER[di], INNER[dj]],
                              field.at[TARGET[di], TARGET[dj]]))
            for n, (source, target, sender) in enumerate(planes):
                kinds.append((9 + 9 * n + k, 1 - off, sender, source.at[SOURCE[di], SOURCE[dj]],
                              target.at[TARGET[di], TARGET[dj]]))
            for slot, to_off, sender, source, target in kinds:
                copy = pltpu.make_async_remote_copy(
                    src_ref=source, dst_ref=target,
                    send_sem=send_sems.at[turn, slot], recv_sem=recv_sems.at[turn, slot],
                    device_id={"off": to_off, "il": il + di, "xl": xl + dj},
                    device_id_type=MESH)
                sends, takes = exists(di, dj), exists(-di, -dj)
                if sender is not None:
                    sends, takes = sends & (off == sender), takes & (off == 1 - sender)
                made.append((sends, takes, copy))
        return made

    def when_all(made, which, act):
        for item in made:
            @pl.when(item[which])
            def _():
                getattr(item[2], act)()

    load = pltpu.make_async_copy(data_ref, dx.at[1:5, 1:5], load_sem)
    load.start()
    load_weight = pltpu.make_async_copy(weight_hbm, weight_ref, weight_sem)
    load_weight.start()
    barrier = pltpu.get_barrier_semaphore()
    for di, dj in STEPS:
        for o in (0, 1):
            if (di, dj, o) != (0, 0, 0):
                @pl.when(exists(di, dj))
                def _():
                    pl.semaphore_signal(
                        barrier, inc=1, device_id_type=MESH,
                        device_id={"off": (off + o) % 2, "il": il + di, "xl": xl + dj})
    rows_near = 1 + (il > 0).astype(jnp.int32) + (il < n_il - 1).astype(jnp.int32)
    cols_near = 1 + (xl > 0).astype(jnp.int32) + (xl < n_xl - 1).astype(jnp.int32)

    full = [(dx, (d0, d1)), (q2x, (q2o,)), (q3x, (q3o,))]
    for field, planes in full:
        for di, dj in STEPS:
            if (di, dj) != (0, 0):
                @pl.when(jnp.logical_not(exists(-di, -dj)))
                def _():
                    shape = field.at[TARGET[di], TARGET[dj]].shape
                    field[TARGET[di], TARGET[dj]] = jnp.zeros(shape, jnp.float32)
                    for plane in planes:
                        shape = plane.at[TARGET[di], TARGET[dj]].shape
                        plane[TARGET[di], TARGET[dj]] = jnp.zeros(shape, jnp.float32)

    load_weight.wait()
    total = weight_ref[0]
    for h in range(1, 8):
        total = total + weight_ref[h]
    wsum[0] = jnp.full((8, 128), total, jnp.float32)
    load.wait()
    for i in range(4):
        for j in range(4):
            tile = dx[1 + i, 1 + j]
            p0[i, j:j + 1] = jnp.where(first, tile[7:8], tile[0:1])
            p1[i, j:j + 1] = tile[1:2]
    pl.semaphore_wait(barrier, 2 * rows_near * cols_near - 1)

    partner = {"off": 1 - off, "il": il, "xl": xl}
    round1 = transfers(0, dx, [(p0, d0, None), (p1, d1, 1)])
    when_all(round1, 0, "start")
    sums = pltpu.make_async_remote_copy(
        src_ref=wsum.at[0], dst_ref=wsum.at[1], send_sem=sum_sems.at[0], recv_sem=sum_sems.at[1],
        device_id=partner, device_id_type=MESH)
    sums.start()
    when_all(round1, 1, "wait_recv")

    @pl.when(off == 1)
    def _():
        for i in range(6):
            for j in range(6):
                d1[i, j:j + 1] = dx[i, j, 0:1]

    keep_next = jnp.where(first, 1.0, 0.0)
    keep_before = 1.0 - keep_next
    row8 = lax.broadcasted_iota(jnp.int32, (8, T), 0)

    def gradients(i, carry):
        for j in range(6):
            d = dx[i, j]
            edge = jnp.broadcast_to(d0[i, j:j + 1] * keep_next, (8, T))
            f = jnp.where(row8 == 7, edge, pltpu.roll(d, 7, 0))
            r = f - d
            s = d + f
            g = 0.25 * (later(s, 1) - earlier(s, 1))
            gg[i, j] = g * g
            gr[i, j] = g * r
            grad[i, j] = g
            res[i, j] = r
        d, f = d0[i], d1[i]
        s = d + f
        g = 0.25 * (later(s, 1) - earlier(s, 1))
        hgg[i] = g * g
        hgr[i] = g * (f - d)
        return carry

    lax.fori_loop(0, 6, gradients, 0)

    row = lax.broadcasted_iota(jnp.int32, (8, 128), 0)

    def smooth_space(field, plane, out):
        def column(c, carry):
            lanes = pl.ds(pl.multiple_of(c * 128, 128), 128)
            sums = []
            for i in range(6):
                tiles = [field[i, j, :, lanes] for j in range(6)]
                pairs = [tiles[j] + tiles[j + 1] for j in range(5)]
                sums.append([pairs[j] + pairs[j + 1] for j in range(4)])
            halo = [plane[i, :, lanes] for i in range(6)]
            for i in range(4):
                h = halo[i] + 2.0 * halo[i + 1] + halo[i + 2]
                h = pltpu.roll(h, 1, 0) + 2.0 * h + pltpu.roll(h, 7, 0)
                before = h * keep_before
                after = h * keep_next
                for j in range(4):
                    x = sums[i][j] + 2.0 * sums[i + 1][j] + sums[i + 2][j]
                    up = jnp.broadcast_to(before[j + 1:j + 2], (8, 128))
                    down = jnp.broadcast_to(after[j + 1:j + 2], (8, 128))
                    up = jnp.where(row == 0, up, pltpu.roll(x, 1, 0))
                    down = jnp.where(row == 7, down, pltpu.roll(x, 7, 0))
                    out[i, j, :, lanes] = up + 2.0 * x + down
            return carry
        lax.fori_loop(0, 8, column, 0)

    def smooth_time(u):
        return (earlier(u, 1) + 2.0 * u + later(u, 1)) * (1.0 / 256.0)

    smooth_space(gg, hgg, ub)
    smooth_space(gr, hgr, uc)

    def start_slope(i, carry):
        for j in range(4):
            inverse = 1.0 / (smooth_time(ub[i, j]) + damping)
            rden[i, j] = inverse
            slope = -smooth_time(uc[i, j]) * inverse
            slopes[i, j] = slope
            g = grad[i + 1, j + 1]
            q = g * (res[i + 1, j + 1] + slope * g)
            q2x[i + 1, j + 1] = q
            pq[0, i, j:j + 1] = jnp.where(first, q[7:8], q[0:1])
        return carry

    lax.fori_loop(0, 4, start_slope, 0)
    round2 = transfers(1, q2x, [(pq.at[0], q2o, None)])
    when_all(round2, 0, "start")
    when_all(round2, 1, "wait_recv")
    smooth_space(q2x, q2o, ub)

    def next_slope(i, carry):
        for j in range(4):
            slope = slopes[i, j] - smooth_time(ub[i, j]) * rden[i, j]
            slopes[i, j] = slope
            g = grad[i + 1, j + 1]
            q = g * (res[i + 1, j + 1] + slope * g)
            q3x[i + 1, j + 1] = q
            pq[1, i, j:j + 1] = jnp.where(first, q[7:8], q[0:1])
        return carry

    lax.fori_loop(0, 4, next_slope, 0)
    round3 = transfers(2, q3x, [(pq.at[1], q3o, None)])
    when_all(round3, 0, "start")
    when_all(round3, 1, "wait_recv")
    smooth_space(q3x, q3o, ub)

    tt = lax.broadcasted_iota(jnp.int32, (8, T), 1).astype(jnp.float32) + 1.0
    hh = lax.broadcasted_iota(jnp.int32, (8, T), 0).astype(jnp.float32) + 0.5
    hh = hh + jnp.where(first, 0.0, 8.0)
    tth = tt * hh
    ttq = tt * tt
    weight = jnp.full((8, 128), weight_ref[0], jnp.float32)
    for h in range(1, 8):
        weight = jnp.where(row == h, weight_ref[h], weight)
    weight = jnp.concatenate([weight] * 8, axis=1)
    high = lax.broadcasted_iota(jnp.int32, (NA, 128), 0)
    high = jnp.where(high < 8, 2 * high, 2 * high - 15)
    high = high.astype(jnp.float32).astype(jnp.bfloat16)
    low = lax.broadcasted_iota(jnp.int32, (NB, 128), 0).astype(jnp.float32).astype(jnp.bfloat16)
    zero_a = jnp.zeros((NA, 128), jnp.bfloat16)
    zero_b = jnp.zeros((NB, 128), jnp.bfloat16)
    one_b = jnp.ones((NB, 128), jnp.bfloat16)
    lane = lax.broadcasted_iota(jnp.int32, (8, 128), 1)

    def push(i, j, at):
        slope = slopes[i, j] - smooth_time(ub[i, j]) * rden[i, j]
        slopes[i, j] = slope
        place = jnp.sqrt(jnp.maximum(ttq - tth * slope, 1.0)) - 1.0
        cell = jnp.floor(place)
        f = place - cell
        cell = jnp.minimum(cell, float(T))
        a = jnp.floor(cell * (1.0 / NB))
        b = cell - a * NB
        v = dx[1 + i, 1 + j] * weight
        x1 = v * f
        x0 = v - x1
        x0h = x0.astype(jnp.bfloat16).astype(jnp.float32)
        x1h = x1.astype(jnp.bfloat16).astype(jnp.float32)
        values = (x0h, x0 - x0h, x1h, x1 - x1h)
        acc = jnp.zeros((4 * NA, NB), jnp.float32)
        for h in range(8):
            left, right = [], []
            for c in range(0, T, 128):
                def spread(x, n):
                    part_of = x[h:h + 1, c:c + 128]
                    return jnp.broadcast_to(part_of, (n, 128)).astype(jnp.bfloat16)
                hit = spread(a, NA) == high
                left.append(jnp.concatenate(
                    [jnp.where(hit, spread(x, NA), zero_a) for x in values], axis=0))
                right.append(jnp.where(spread(b, NB) == low, one_b, zero_b))
            dot = lax.dot_general(
                jnp.concatenate(left, axis=1), jnp.concatenate(right, axis=1),
                (((1,), (1,)), ((), ())), preferred_element_type=jnp.float32)
            acc = acc + jnp.maximum(dot, -3.0e38)
        raw[at] = acc

    def gather(at):
        acc = raw[at]
        lower = acc[:NA] + acc[NA:2 * NA]
        upper = acc[2 * NA:3 * NA] + acc[3 * NA:]
        lower = jnp.concatenate([lower[:8], lower[8:]], axis=1)
        upper = jnp.concatenate([upper[:8], upper[8:]], axis=1)
        upper = pltpu.roll(upper, 1, 1)
        before = pltpu.roll(upper, 1, 0)
        upper = jnp.where(lane == 0, jnp.where(row == 0, 0.0, before), upper)
        part[0, at] = lower + upper

    def exchange(n):
        return pltpu.make_async_remote_copy(
            src_ref=part.at[0, 4 * n:4 * n + 4], dst_ref=part.at[1, 4 * n:4 * n + 4],
            send_sem=part_sems.at[0, n], recv_sem=part_sems.at[1, n],
            device_id=partner, device_id_type=MESH)

    def store(i):
        return pltpu.make_async_copy(slopes.at[i], out_ref.at[i], slope_sems.at[i])

    def push_row(i, carry):
        for j in range(4):
            push(i, j, 4 * i + j)
        store(i).start()
        return carry

    lax.fori_loop(0, 4, push_row, 0)
    for n in range(4):
        for at in range(4 * n, 4 * n + 4):
            gather(at)
        exchange(n).start()
    sums.wait_recv()
    weights = wsum[0] + wsum[1]
    for n in range(4):
        exchange(n).wait_recv()
        for at in range(4 * n, 4 * n + 4):
            stack_ref[at] = (part[0, at] + part[1, at]) / weights
    sums.wait_send()
    for n in range(4):
        exchange(n).wait_send()
        store(n).wait()
    for made in (round1, round2, round3):
        when_all(made, 0, "wait_send")


def moveout(data, offset_weight, counts):
    tiles = pltpu.VMEM((6, 6, 8, T), jnp.float32)
    plane = pltpu.VMEM((6, 8, T), jnp.float32)
    own = pltpu.VMEM((4, 4, 8, T), jnp.float32)
    rows = pltpu.VMEM((4, 8, T), jnp.float32)
    return pl.pallas_call(
        lambda *refs: moveout_kernel(counts, *refs),
        out_shape=(jax.ShapeDtypeStruct((4, 4, 8, T), jnp.float32),
                   jax.ShapeDtypeStruct((16, 8, 128), jnp.float32)),
        in_specs=[pl.BlockSpec(memory_space=pltpu.HBM)] * 2,
        out_specs=(pl.BlockSpec(memory_space=pltpu.HBM), pl.BlockSpec(memory_space=pltpu.VMEM)),
        scratch_shapes=[tiles, plane, plane, rows, rows, tiles, tiles, plane, plane, tiles, tiles,
                        own, own, own, tiles, plane, tiles, plane,
                        pltpu.VMEM((2, 4, 8, T), jnp.float32),
                        pltpu.VMEM((2, 8, 128), jnp.float32),
                        pltpu.VMEM((16, 4 * NA, NB), jnp.float32),
                        pltpu.VMEM((2, 16, 8, 128), jnp.float32),
                        pltpu.SemaphoreType.DMA, pltpu.SemaphoreType.DMA((3, 27)),
                        pltpu.SemaphoreType.DMA((3, 27)), pltpu.SemaphoreType.DMA((2,)),
                        pltpu.SemaphoreType.DMA((2, 4)), pltpu.SMEM((8,), jnp.float32),
                        pltpu.SemaphoreType.DMA, own, pltpu.SemaphoreType.DMA((4,))],
        compiler_params=pltpu.CompilerParams(
            collective_id=0, has_side_effects=True, vmem_limit_bytes=67043328),
        name="moveout",
    )(offset_weight, data)


def solution(mesh):
    counts = (mesh.shape["il"], mesh.shape["xl"])

    def shards(data, offset_weight):
        slope, stacked = moveout(data, offset_weight, counts)
        return slope, stacked.reshape(4, 4, T)

    return jax.shard_map(
        shards,
        mesh=mesh,
        in_specs=(P("il", "xl", "off", None), P("off")),
        out_specs=(P("il", "xl", "off", None), P("il", "xl", None)),
        check_vma=False,
    )
```

```python
import jax
import jax.numpy as jnp
from jax import lax
from jax.experimental import pallas as pl
from jax.experimental.pallas import tpu as pltpu
from jax.sharding import PartitionSpec as P

T = 1024
NA = 16
NB = 64
damping = 0.05
MESH = pl.DeviceIdType.MESH
STEPS = [(di, dj) for di in (-1, 0, 1) for dj in (-1, 0, 1)]
SOURCE = {-1: slice(0, 1), 0: slice(0, 4), 1: slice(3, 4)}
INNER = {-1: slice(1, 2), 0: slice(1, 5), 1: slice(4, 5)}
TARGET = {-1: slice(5, 6), 0: slice(1, 5), 1: slice(0, 1)}
WINDOWS = ((0, 512), (384, 640))
SEAM = 448


def earlier(x, axis):
    x = pltpu.roll(x, 1, axis)
    at = lax.broadcasted_iota(jnp.int32, (8, 128), axis)
    return jnp.concatenate([jnp.where(at == 0, 0.0, x[:, :128]), x[:, 128:]], axis=1)


def later(x, axis):
    n = x.shape[axis]
    x = pltpu.roll(x, n - 1, axis)
    at = lax.broadcasted_iota(jnp.int32, (8, 128), axis)
    return jnp.concatenate([x[:, :n - 128], jnp.where(at == 127, 0.0, x[:, n - 128:])], axis=1)


def smooth_time(u):
    return (earlier(u, 1) + 2.0 * u + later(u, 1)) * (1.0 / 256.0)


def moveout_kernel(counts, weight_hbm, data_hbm, out_ref, stack_ref, *scratch):
    halves, scratch = (scratch[:20], scratch[20:40]), scratch[40:]
    (wsum, raw, part, weight_ref, weight_sem, load_sems, send_sems, recv_sems,
     sum_sems, part_sems) = scratch
    n_il, n_xl = counts
    off, il, xl = lax.axis_index("off"), lax.axis_index("il"), lax.axis_index("xl")
    first = off == 0
    partner = {"off": 1 - off, "il": il, "xl": xl}

    def exists(di, dj):
        i, j = il + di, xl + dj
        return (i >= 0) & (i < n_il) & (j >= 0) & (j < n_xl)

    def transfers(turn, field, planes):
        made = []
        for k, (di, dj) in enumerate(STEPS):
            kinds = []
            if (di, dj) != (0, 0):
                kinds.append((k, off, None, field.at[INNER[di], INNER[dj]],
                              field.at[TARGET[di], TARGET[dj]]))
            for n, (source, target, sender) in enumerate(planes):
                kinds.append((9 + 9 * n + k, 1 - off, sender, source.at[SOURCE[di], SOURCE[dj]],
                              target.at[TARGET[di], TARGET[dj]]))
            for slot, to_off, sender, source, target in kinds:
                copy = pltpu.make_async_remote_copy(
                    src_ref=source, dst_ref=target,
                    send_sem=send_sems.at[turn, slot], recv_sem=recv_sems.at[turn, slot],
                    device_id={"off": to_off, "il": il + di, "xl": xl + dj},
                    device_id_type=MESH)
                sends, takes = exists(di, dj), exists(-di, -dj)
                if sender is not None:
                    sends, takes = sends & (off == sender), takes & (off == 1 - sender)
                made.append((sends, takes, copy))
        return made

    def when_all(made, which, act):
        for item in made:
            @pl.when(item[which])
            def _():
                getattr(item[2], act)()

    loads = []
    for n, (base, width) in enumerate(WINDOWS):
        load = pltpu.make_async_copy(
            data_hbm.at[:, :, :, base:base + width], halves[n][0].at[1:5, 1:5], load_sems.at[n])
        load.start()
        loads.append(load)
    load_weight = pltpu.make_async_copy(weight_hbm, weight_ref, weight_sem)
    load_weight.start()
    barrier = pltpu.get_barrier_semaphore()
    for di, dj in STEPS:
        for o in (0, 1):
            if (di, dj, o) != (0, 0, 0):
                @pl.when(exists(di, dj))
                def _():
                    pl.semaphore_signal(
                        barrier, inc=1, device_id_type=MESH,
                        device_id={"off": (off + o) % 2, "il": il + di, "xl": xl + dj})
    rows_near = 1 + (il > 0).astype(jnp.int32) + (il < n_il - 1).astype(jnp.int32)
    cols_near = 1 + (xl > 0).astype(jnp.int32) + (xl < n_xl - 1).astype(jnp.int32)

    for dx, d0, d1, _, _, gg, gr, hgg, hgr, grad, res, rden, ub, uc, q2, o2, q3, o3, pq, own \
            in halves:
        for field, planes in ((dx, (d0, d1)), (q2, (o2,)), (q3, (o3,))):
            for di, dj in STEPS:
                if (di, dj) != (0, 0):
                    @pl.when(jnp.logical_not(exists(-di, -dj)))
                    def _():
                        for target in (field,) + planes:
                            shape = target.at[TARGET[di], TARGET[dj]].shape
                            target[TARGET[di], TARGET[dj]] = jnp.zeros(shape, jnp.float32)

    load_weight.wait()
    total = weight_ref[0]
    for h in range(1, 8):
        total = total + weight_ref[h]
    wsum[0] = jnp.full((8, 128), total, jnp.float32)
    for load, half in zip(loads, halves):
        load.wait()
        dx, p0, p1 = half[0], half[3], half[4]
        for i in range(4):
            for j in range(4):
                tile = dx[1 + i, 1 + j]
                p0[i, j:j + 1] = jnp.where(first, tile[7:8], tile[0:1])
                p1[i, j:j + 1] = tile[1:2]
    pl.semaphore_wait(barrier, 2 * rows_near * cols_near - 1)

    rounds = []
    for n, half in enumerate(halves):
        dx, d0, d1, p0, p1 = half[:5]
        made = transfers(n, dx, [(p0, d0, None), (p1, d1, 1)])
        when_all(made, 0, "start")
        rounds.append(made)
    sums = pltpu.make_async_remote_copy(
        src_ref=wsum.at[0], dst_ref=wsum.at[1], send_sem=sum_sems.at[0], recv_sem=sum_sems.at[1],
        device_id=partner, device_id_type=MESH)
    sums.start()

    keep_next = jnp.where(first, 1.0, 0.0)
    keep_before = 1.0 - keep_next
    row = lax.broadcasted_iota(jnp.int32, (8, 128), 0)
    lane = lax.broadcasted_iota(jnp.int32, (8, 128), 1)

    def smooth_space(field, plane, out):
        def column(c, carry):
            lanes = pl.ds(pl.multiple_of(c * 128, 128), 128)
            sums_xl = []
            for i in range(6):
                tiles = [field[i, j, :, lanes] for j in range(6)]
                pairs = [tiles[j] + tiles[j + 1] for j in range(5)]
                sums_xl.append([pairs[j] + pairs[j + 1] for j in range(4)])
            halo = [plane[i, :, lanes] for i in range(6)]
            for i in range(4):
                h = halo[i] + 2.0 * halo[i + 1] + halo[i + 2]
                h = pltpu.roll(h, 1, 0) + 2.0 * h + pltpu.roll(h, 7, 0)
                before = h * keep_before
                after = h * keep_next
                for j in range(4):
                    x = sums_xl[i][j] + 2.0 * sums_xl[i + 1][j] + sums_xl[i + 2][j]
                    up = jnp.broadcast_to(before[j + 1:j + 2], (8, 128))
                    down = jnp.broadcast_to(after[j + 1:j + 2], (8, 128))
                    up = jnp.where(row == 0, up, pltpu.roll(x, 1, 0))
                    down = jnp.where(row == 7, down, pltpu.roll(x, 7, 0))
                    out[i, j, :, lanes] = up + 2.0 * x + down
            return carry
        lax.fori_loop(0, field.shape[3] // 128, column, 0)

    def first_turn(n):
        dx, d0, d1, _, _, gg, gr, hgg, hgr, grad, res, rden, ub, uc, q2, o2, q3, o3, pq, own = \
            halves[n]
        width = WINDOWS[n][1]
        row8 = lax.broadcasted_iota(jnp.int32, (8, width), 0)

        @pl.when(off == 1)
        def _():
            for i in range(6):
                for j in range(6):
                    d1[i, j:j + 1] = dx[i, j, 0:1]

        def gradients(i, carry):
            for j in range(6):
                d = dx[i, j]
                edge = jnp.broadcast_to(d0[i, j:j + 1] * keep_next, (8, width))
                f = jnp.where(row8 == 7, edge, pltpu.roll(d, 7, 0))
                r = f - d
                s = d + f
                g = 0.25 * (later(s, 1) - earlier(s, 1))
                gg[i, j] = g * g
                gr[i, j] = g * r
                grad[i, j] = g
                res[i, j] = r
            d, f = d0[i], d1[i]
            s = d + f
            g = 0.25 * (later(s, 1) - earlier(s, 1))
            hgg[i] = g * g
            hgr[i] = g * (f - d)
            return carry

        lax.fori_loop(0, 6, gradients, 0)
        smooth_space(gg, hgg, ub)
        smooth_space(gr, hgr, uc)

        def start_slope(i, carry):
            for j in range(4):
                inverse = 1.0 / (smooth_time(ub[i, j]) + damping)
                rden[i, j] = inverse
                slope = -smooth_time(uc[i, j]) * inverse
                own[i, j] = slope
                g = grad[i + 1, j + 1]
                q = g * (res[i + 1, j + 1] + slope * g)
                q2[i + 1, j + 1] = q
                pq[0, i, j:j + 1] = jnp.where(first, q[7:8], q[0:1])
            return carry

        lax.fori_loop(0, 4, start_slope, 0)
        made = transfers(2 + n, q2, [(pq.at[0], o2, None)])
        when_all(made, 0, "start")
        rounds.append(made)

    def second_turn(n):
        grad, res, rden, ub, q2, o2, q3, pq, own = (halves[n][k] for k in (
            9, 10, 11, 12, 14, 15, 16, 18, 19))
        smooth_space(q2, o2, ub)

        def next_slope(i, carry):
            for j in range(4):
                slope = own[i, j] - smooth_time(ub[i, j]) * rden[i, j]
                own[i, j] = slope
                g = grad[i + 1, j + 1]
                q = g * (res[i + 1, j + 1] + slope * g)
                q3[i + 1, j + 1] = q
                pq[1, i, j:j + 1] = jnp.where(first, q[7:8], q[0:1])
            return carry

        lax.fori_loop(0, 4, next_slope, 0)
        made = transfers(4 + n, q3, [(pq.at[1], halves[n][17], None)])
        when_all(made, 0, "start")
        rounds.append(made)

    weight = jnp.full((8, 128), weight_ref[0], jnp.float32)
    for h in range(1, 8):
        weight = jnp.where(row == h, weight_ref[h], weight)
    high = lax.broadcasted_iota(jnp.int32, (NA, 128), 0)
    high = jnp.where(high < 8, 2 * high, 2 * high - 15)
    high = high.astype(jnp.float32).astype(jnp.bfloat16)
    low = lax.broadcasted_iota(jnp.int32, (NB, 128), 0).astype(jnp.float32).astype(jnp.bfloat16)
    zero_a = jnp.zeros((NA, 128), jnp.bfloat16)
    zero_b = jnp.zeros((NB, 128), jnp.bfloat16)
    one_b = jnp.ones((NB, 128), jnp.bfloat16)

    def push(data, slope, start):
        width = data.shape[1]
        tt = lax.broadcasted_iota(jnp.int32, (8, width), 1).astype(jnp.float32) + (start + 1.0)
        hh = lax.broadcasted_iota(jnp.int32, (8, width), 0).astype(jnp.float32) + 0.5
        hh = hh + 8.0 * keep_before
        place = jnp.sqrt(jnp.maximum(tt * tt - tt * hh * slope, 1.0)) - 1.0
        cell = jnp.floor(place)
        f = place - cell
        cell = jnp.minimum(cell, float(T))
        a = jnp.floor(cell * (1.0 / NB))
        b = cell - a * NB
        v = data * jnp.concatenate([weight] * (width // 128), axis=1)
        x1 = v * f
        x0 = v - x1
        x0h = x0.astype(jnp.bfloat16).astype(jnp.float32)
        x1h = x1.astype(jnp.bfloat16).astype(jnp.float32)
        values = (x0h, x0 - x0h, x1h, x1 - x1h)
        acc = jnp.zeros((4 * NA, NB), jnp.float32)
        for h in range(0, 8, 2):
            left, right = [], []
            for k in (h, h + 1):
                for c in range(0, width, 128):
                    def spread(x, n):
                        piece = x[k:k + 1, c:c + 128]
                        return jnp.broadcast_to(piece, (n, 128)).astype(jnp.bfloat16)
                    hit = spread(a, NA) == high
                    left.append(jnp.concatenate(
                        [jnp.where(hit, spread(x, NA), zero_a) for x in values], axis=0))
                    right.append(jnp.where(spread(b, NB) == low, one_b, zero_b))
            dot = lax.dot_general(
                jnp.concatenate(left, axis=1), jnp.concatenate(right, axis=1),
                (((1,), (1,)), ((), ())), preferred_element_type=jnp.float32)
            acc = acc + jnp.maximum(dot, -3.0e38)
        return acc

    def gather(i):
        for j in range(4):
            acc = raw[4 * i + j]
            lower = acc[:NA] + acc[NA:2 * NA]
            upper = acc[2 * NA:3 * NA] + acc[3 * NA:]
            lower = jnp.concatenate([lower[:8], lower[8:]], axis=1)
            upper = jnp.concatenate([upper[:8], upper[8:]], axis=1)
            upper = pltpu.roll(upper, 1, 1)
            before = pltpu.roll(upper, 1, 0)
            upper = jnp.where(lane == 0, jnp.where(row == 0, 0.0, before), upper)
            part[0, i, j] = lower + upper

    def exchange(i):
        return pltpu.make_async_remote_copy(
            src_ref=part.at[0, i], dst_ref=part.at[1, i],
            send_sem=part_sems.at[0, i], recv_sem=part_sems.at[1, i],
            device_id=partner, device_id_type=MESH)

    def push_first(i, carry):
        dx, rden, ub, own = (halves[0][k] for k in (0, 11, 12, 19))
        for j in range(4):
            slope = own[i, j] - smooth_time(ub[i, j]) * rden[i, j]
            own[i, j] = slope
            out_ref[i, j, :, :384] = slope[:, :384]
            raw[4 * i + j] = push(dx[i + 1, j + 1, :, :384], slope[:, :384], 0.0)
        return carry

    def push_second(i):
        dx, rden, ub, own = (halves[1][k] for k in (0, 11, 12, 19))
        for j in range(4):
            slope = own[i, j] - smooth_time(ub[i, j]) * rden[i, j]
            seam = jnp.where(lane < SEAM - 384, halves[0][19][i, j, :, 384:], slope[:, :128])
            slope = jnp.concatenate([seam, slope[:, 128:]], axis=1)
            out_ref[i, j, :, 384:] = slope
            raw[4 * i + j] = raw[4 * i + j] + push(dx[i + 1, j + 1], slope, 384.0)

    for turn, act in enumerate((first_turn, second_turn)):
        for n in (0, 1):
            when_all(rounds[2 * turn + n], 1, "wait_recv")
            act(n)
    when_all(rounds[4], 1, "wait_recv")
    smooth_space(halves[0][16], halves[0][17], halves[0][12])
    lax.fori_loop(0, 4, push_first, 0)
    when_all(rounds[5], 1, "wait_recv")
    smooth_space(halves[1][16], halves[1][17], halves[1][12])
    push_second(0)

    def push_rest(i, carry):
        gather(i - 1)
        push_second(i)
        exchange(i - 1).start()
        return carry

    lax.fori_loop(1, 4, push_rest, 0)
    gather(3)
    exchange(3).start()
    sums.wait_recv()
    weights = wsum[0] + wsum[1]
    for i in range(4):
        exchange(i).wait_recv()
        for j in range(4):
            stacked = (part[0, i, j] + part[1, i, j]) / weights
            for r in range(8):
                stack_ref[i, j:j + 1, 128 * r:128 * r + 128] = stacked[r:r + 1]
    sums.wait_send()
    for i in range(4):
        exchange(i).wait_send()
    for made in rounds:
        when_all(made, 0, "wait_send")


def moveout(data, offset_weight, counts):
    scratch = []
    for _, width in WINDOWS:
        tiles = pltpu.VMEM((6, 6, 8, width), jnp.float32)
        plane = pltpu.VMEM((6, 8, width), jnp.float32)
        own = pltpu.VMEM((4, 4, 8, width), jnp.float32)
        rows = pltpu.VMEM((4, 8, width), jnp.float32)
        scratch += [tiles, plane, plane, rows, rows, tiles, tiles, plane, plane, tiles, tiles,
                    own, own, own, tiles, plane, tiles, plane,
                    pltpu.VMEM((2, 4, 8, width), jnp.float32), own]
    return pl.pallas_call(
        lambda *refs: moveout_kernel(counts, *refs),
        out_shape=(jax.ShapeDtypeStruct((4, 4, 8, T), jnp.float32),
                   jax.ShapeDtypeStruct((4, 4, T), jnp.float32)),
        in_specs=[pl.BlockSpec(memory_space=pltpu.HBM)] * 2,
        out_specs=(pl.BlockSpec(memory_space=pltpu.VMEM), pl.BlockSpec(memory_space=pltpu.VMEM)),
        scratch_shapes=scratch + [
            pltpu.VMEM((2, 8, 128), jnp.float32),
            pltpu.VMEM((16, 4 * NA, NB), jnp.float32),
            pltpu.VMEM((2, 4, 4, 8, 128), jnp.float32),
            pltpu.SMEM((8,), jnp.float32), pltpu.SemaphoreType.DMA,
            pltpu.SemaphoreType.DMA((2,)), pltpu.SemaphoreType.DMA((6, 27)),
            pltpu.SemaphoreType.DMA((6, 27)), pltpu.SemaphoreType.DMA((2,)),
            pltpu.SemaphoreType.DMA((2, 4))],
        compiler_params=pltpu.CompilerParams(
            collective_id=0, has_side_effects=True, vmem_limit_bytes=48 * 2**20),
        name="moveout",
    )(pltpu.with_memory_space_constraint(offset_weight, pltpu.HBM),
      pltpu.with_memory_space_constraint(data, pltpu.HBM))


def solution(mesh):
    counts = (mesh.shape["il"], mesh.shape["xl"])
    return jax.shard_map(
        lambda data, offset_weight: moveout(data, offset_weight, counts),
        mesh=mesh,
        in_specs=(P("il", "xl", "off", None), P("off")),
        out_specs=(P("il", "xl", "off", None), P("il", "xl", None)),
        check_vma=False,
    )
```

```python
import jax
import jax.numpy as jnp
from jax import lax
from jax.experimental import pallas as pl
from jax.experimental.pallas import tpu as pltpu
from jax.sharding import PartitionSpec as P

T = 1024
NA = 16
NB = 64
damping = 0.05
MESH = pl.DeviceIdType.MESH
STEPS = [(di, dj) for di in (-1, 0, 1) for dj in (-1, 0, 1)]
SOURCE = {-1: slice(0, 1), 0: slice(0, 4), 1: slice(3, 4)}
INNER = {-1: slice(1, 2), 0: slice(1, 5), 1: slice(4, 5)}
TARGET = {-1: slice(5, 6), 0: slice(1, 5), 1: slice(0, 1)}
WINDOWS = ((0, 512), (384, 640))
SEAM = 448


def earlier(x, axis):
    x = pltpu.roll(x, 1, axis)
    at = lax.broadcasted_iota(jnp.int32, (8, 128), axis)
    return jnp.concatenate([jnp.where(at == 0, 0.0, x[:, :128]), x[:, 128:]], axis=1)


def later(x, axis):
    n = x.shape[axis]
    x = pltpu.roll(x, n - 1, axis)
    at = lax.broadcasted_iota(jnp.int32, (8, 128), axis)
    return jnp.concatenate([x[:, :n - 128], jnp.where(at == 127, 0.0, x[:, n - 128:])], axis=1)


def smooth_time(u):
    return (earlier(u, 1) + 2.0 * u + later(u, 1)) * (1.0 / 256.0)


def moveout_kernel(counts, weight_hbm, data_hbm, out_ref, stack_ref, *scratch):
    halves, scratch = (scratch[:20], scratch[20:40]), scratch[40:]
    (wsum, raw, part, weight_ref, weight_sem, load_sems, send_sems, recv_sems,
     sum_sems, part_sems) = scratch
    n_il, n_xl = counts
    off, il, xl = lax.axis_index("off"), lax.axis_index("il"), lax.axis_index("xl")
    first = off == 0
    partner = {"off": 1 - off, "il": il, "xl": xl}

    def exists(di, dj):
        i, j = il + di, xl + dj
        return (i >= 0) & (i < n_il) & (j >= 0) & (j < n_xl)

    def transfers(turn, field, planes):
        made = []
        for k, (di, dj) in enumerate(STEPS):
            def copy(slot, to_off, source, target):
                return pltpu.make_async_remote_copy(
                    src_ref=source, dst_ref=target,
                    send_sem=send_sems.at[turn, slot], recv_sem=recv_sems.at[turn, slot],
                    device_id={"off": to_off, "il": il + di, "xl": xl + dj},
                    device_id_type=MESH)
            sends, takes = exists(di, dj), exists(-di, -dj)
            copies = []
            if field is not None and (di, dj) != (0, 0):
                copies.append(copy(k, off, field.at[INNER[di], INNER[dj]],
                                   field.at[TARGET[di], TARGET[dj]]))
            for n, (source, target) in enumerate(planes):
                plane = copy(9 + 9 * n + k, 1 - off, source.at[SOURCE[di], SOURCE[dj]],
                             target.at[TARGET[di], TARGET[dj]])
                if n == 0:
                    copies.append(plane)
                else:
                    made.append((sends & (off == 1), takes & first, [plane], 18 + k))
            if copies:
                made.append((sends, takes, copies, 9 + k))
        return made

    def when_all(made, which, act):
        for item in made:
            @pl.when(item[which])
            def _():
                for copy in item[2]:
                    getattr(copy, act)()

    loads = []
    for n, (base, width) in enumerate(WINDOWS):
        load = pltpu.make_async_copy(
            data_hbm.at[:, :, :, base:base + width], halves[n][0].at[1:5, 1:5], load_sems.at[n])
        load.start()
        loads.append(load)
    load_weight = pltpu.make_async_copy(weight_hbm, weight_ref, weight_sem)
    load_weight.start()
    barrier = pltpu.get_barrier_semaphore()
    for di, dj in STEPS:
        for o in (0, 1):
            if (di, dj, o) != (0, 0, 0):
                @pl.when(exists(di, dj))
                def _():
                    pl.semaphore_signal(
                        barrier, inc=1, device_id_type=MESH,
                        device_id={"off": (off + o) % 2, "il": il + di, "xl": xl + dj})
    rows_near = 1 + (il > 0).astype(jnp.int32) + (il < n_il - 1).astype(jnp.int32)
    cols_near = 1 + (xl > 0).astype(jnp.int32) + (xl < n_xl - 1).astype(jnp.int32)

    load_weight.wait()
    total = weight_ref[0]
    for h in range(1, 8):
        total = total + weight_ref[h]
    wsum[0] = jnp.full((8, 128), total, jnp.float32)
    for load in loads:
        load.wait()
    pl.semaphore_wait(barrier, 2 * rows_near * cols_near - 1)

    rounds = []
    for n, half in enumerate(halves):
        dx, d0, d1, p0, p1 = half[:5]
        made = transfers(n, dx, [])
        when_all(made, 0, "start")
        for i in range(4):
            for j in range(4):
                tile = dx[1 + i, 1 + j]
                p0[i, j:j + 1] = jnp.where(first, tile[7:8], tile[0:1])
                p1[i, j:j + 1] = tile[1:2]
        plane = transfers(n, None, [(p0, d0), (p1, d1)])
        when_all(plane, 0, "start")
        rounds.append((made, plane))
    sums = pltpu.make_async_remote_copy(
        src_ref=wsum.at[0], dst_ref=wsum.at[1], send_sem=sum_sems.at[0], recv_sem=sum_sems.at[1],
        device_id=partner, device_id_type=MESH)
    sums.start()

    for di, dj in STEPS:
        if (di, dj) != (0, 0):
            @pl.when(jnp.logical_not(exists(-di, -dj)))
            def _():
                for half in halves:
                    for n in (0, 1, 2, 14, 15, 16, 17):
                        shape = half[n].at[TARGET[di], TARGET[dj]].shape
                        half[n][TARGET[di], TARGET[dj]] = jnp.zeros(shape, jnp.float32)

    keep_next = jnp.where(first, 1.0, 0.0)
    keep_before = 1.0 - keep_next
    row = lax.broadcasted_iota(jnp.int32, (8, 128), 0)
    lane = lax.broadcasted_iota(jnp.int32, (8, 128), 1)

    def smooth_space(field, plane, out):
        def column(c, carry):
            lanes = pl.ds(pl.multiple_of(c * 128, 128), 128)
            sums_xl = []
            for i in range(6):
                tiles = [field[i, j, :, lanes] for j in range(6)]
                pairs = [tiles[j] + tiles[j + 1] for j in range(5)]
                sums_xl.append([pairs[j] + pairs[j + 1] for j in range(4)])
            halo = [plane[i, :, lanes] for i in range(6)]
            for i in range(4):
                h = halo[i] + 2.0 * halo[i + 1] + halo[i + 2]
                h = pltpu.roll(h, 1, 0) + 2.0 * h + pltpu.roll(h, 7, 0)
                before = h * keep_before
                after = h * keep_next
                for j in range(4):
                    x = sums_xl[i][j] + 2.0 * sums_xl[i + 1][j] + sums_xl[i + 2][j]
                    up = jnp.broadcast_to(before[j + 1:j + 2], (8, 128))
                    down = jnp.broadcast_to(after[j + 1:j + 2], (8, 128))
                    up = jnp.where(row == 0, up, pltpu.roll(x, 1, 0))
                    down = jnp.where(row == 7, down, pltpu.roll(x, 7, 0))
                    out[i, j, :, lanes] = up + 2.0 * x + down
            return carry
        lax.fori_loop(0, field.shape[3] // 128, column, 0)

    def first_turn(n, inner):
        dx, d0, d1, _, _, gg, gr, hgg, hgr, grad, res, rden, ub, uc, q2, o2, q3, o3, pq, own = \
            halves[n]
        width = WINDOWS[n][1]
        row8 = lax.broadcasted_iota(jnp.int32, (8, width), 0)

        def gradients(i, j):
            d = dx[i, j]
            edge = jnp.broadcast_to(d0[i, j:j + 1] * keep_next, (8, width))
            f = jnp.where(row8 == 7, edge, pltpu.roll(d, 7, 0))
            r = f - d
            s = d + f
            g = 0.25 * (later(s, 1) - earlier(s, 1))
            gg[i, j] = g * g
            gr[i, j] = g * r
            grad[i, j] = g
            res[i, j] = r

        made, plane = rounds[n]
        if inner:
            centre = [item for item in plane if item[3] == 13]
            when_all(centre, 1, "wait_recv")
            for i in range(1, 5):
                for j in range(1, 5):
                    gradients(i, j)
            return
        when_all(made + [item for item in plane if item[3] != 13], 1, "wait_recv")

        @pl.when(off == 1)
        def _():
            for i in range(6):
                for j in range(6):
                    d1[i, j:j + 1] = dx[i, j, 0:1]

        for i in range(6):
            for j in range(6):
                if i in (0, 5) or j in (0, 5):
                    gradients(i, j)
            d, f = d0[i], d1[i]
            s = d + f
            g = 0.25 * (later(s, 1) - earlier(s, 1))
            hgg[i] = g * g
            hgr[i] = g * (f - d)

        smooth_space(gg, hgg, ub)
        smooth_space(gr, hgr, uc)

        def start_slope(i, carry):
            for j in range(4):
                inverse = 1.0 / (smooth_time(ub[i, j]) + damping)
                rden[i, j] = inverse
                slope = -smooth_time(uc[i, j]) * inverse
                own[i, j] = slope
                g = grad[i + 1, j + 1]
                q = g * (res[i + 1, j + 1] + slope * g)
                q2[i + 1, j + 1] = q
                pq[0, i, j:j + 1] = jnp.where(first, q[7:8], q[0:1])
            return carry

        lax.fori_loop(0, 4, start_slope, 0, unroll=2)
        made = transfers(2 + n, q2, [(pq.at[0], o2)])
        when_all(made, 0, "start")
        rounds.append(made)

    def second_turn(n):
        grad, res, rden, ub, q2, o2, q3, pq, own = (halves[n][k] for k in (
            9, 10, 11, 12, 14, 15, 16, 18, 19))
        smooth_space(q2, o2, ub)

        def next_slope(i, carry):
            for j in range(4):
                slope = own[i, j] - smooth_time(ub[i, j]) * rden[i, j]
                own[i, j] = slope
                g = grad[i + 1, j + 1]
                q = g * (res[i + 1, j + 1] + slope * g)
                q3[i + 1, j + 1] = q
                pq[1, i, j:j + 1] = jnp.where(first, q[7:8], q[0:1])
            return carry

        lax.fori_loop(0, 4, next_slope, 0, unroll=4)
        made = transfers(4 + n, q3, [(pq.at[1], halves[n][17])])
        when_all(made, 0, "start")
        rounds.append(made)

    weight = jnp.full((8, 128), weight_ref[0], jnp.float32)
    for h in range(1, 8):
        weight = jnp.where(row == h, weight_ref[h], weight)
    high = lax.broadcasted_iota(jnp.int32, (NA, 128), 0)
    high = jnp.where(high < 8, 2 * high, 2 * high - 15)
    high = high.astype(jnp.float32).astype(jnp.bfloat16)
    low = lax.broadcasted_iota(jnp.int32, (NB, 128), 0).astype(jnp.float32).astype(jnp.bfloat16)
    zero_a = jnp.zeros((NA, 128), jnp.bfloat16)
    zero_b = jnp.zeros((NB, 128), jnp.bfloat16)
    one_b = jnp.ones((NB, 128), jnp.bfloat16)

    def push(data, slope, start):
        width = data.shape[1]
        tt = lax.broadcasted_iota(jnp.int32, (8, width), 1).astype(jnp.float32) + (start + 1.0)
        hh = lax.broadcasted_iota(jnp.int32, (8, width), 0).astype(jnp.float32) + 0.5
        hh = hh + 8.0 * keep_before
        place = jnp.sqrt(jnp.maximum(tt * tt - tt * hh * slope, 1.0)) - 1.0
        cell = jnp.floor(place)
        f = place - cell
        cell = jnp.minimum(cell, float(T))
        a = jnp.floor(cell * (1.0 / NB))
        b = cell - a * NB
        v = data * jnp.concatenate([weight] * (width // 128), axis=1)
        x1 = v * f
        x0 = v - x1
        x0h = x0.astype(jnp.bfloat16).astype(jnp.float32)
        x1h = x1.astype(jnp.bfloat16).astype(jnp.float32)
        values = (x0h, x0 - x0h, x1h, x1 - x1h)
        acc = jnp.zeros((4 * NA, NB), jnp.float32)
        for h in range(0, 8, 2):
            left, right = [], []
            for k in (h, h + 1):
                for c in range(0, width, 128):
                    def spread(x, n):
                        piece = x[k:k + 1, c:c + 128]
                        return jnp.broadcast_to(piece, (n, 128)).astype(jnp.bfloat16)
                    hit = spread(a, NA) == high
                    left.append(jnp.concatenate(
                        [jnp.where(hit, spread(x, NA), zero_a) for x in values], axis=0))
                    right.append(jnp.where(spread(b, NB) == low, one_b, zero_b))
            dot = lax.dot_general(
                jnp.concatenate(left, axis=1), jnp.concatenate(right, axis=1),
                (((1,), (1,)), ((), ())), preferred_element_type=jnp.float32)
            acc = acc + jnp.maximum(dot, -3.0e38)
        return acc

    def gather(i):
        for j in range(4):
            acc = raw[4 * i + j]
            lower = acc[:NA] + acc[NA:2 * NA]
            upper = acc[2 * NA:3 * NA] + acc[3 * NA:]
            lower = jnp.concatenate([lower[:8], lower[8:]], axis=1)
            upper = jnp.concatenate([upper[:8], upper[8:]], axis=1)
            upper = pltpu.roll(upper, 1, 1)
            before = pltpu.roll(upper, 1, 0)
            upper = jnp.where(lane == 0, jnp.where(row == 0, 0.0, before), upper)
            part[0, i, j] = lower + upper

    def exchange(i):
        return pltpu.make_async_remote_copy(
            src_ref=part.at[0, i], dst_ref=part.at[1, i],
            send_sem=part_sems.at[0, i], recv_sem=part_sems.at[1, i],
            device_id=partner, device_id_type=MESH)

    def push_first(i, carry):
        dx, rden, ub, own = (halves[0][k] for k in (0, 11, 12, 19))
        for j in range(4):
            slope = own[i, j] - smooth_time(ub[i, j]) * rden[i, j]
            own[i, j] = slope
            out_ref[i, j, :, :384] = slope[:, :384]
            raw[4 * i + j] = push(dx[i + 1, j + 1, :, :384], slope[:, :384], 0.0)
        return carry

    def push_second(i):
        dx, rden, ub, own = (halves[1][k] for k in (0, 11, 12, 19))
        for j in range(4):
            slope = own[i, j] - smooth_time(ub[i, j]) * rden[i, j]
            seam = jnp.where(lane < SEAM - 384, halves[0][19][i, j, :, 384:], slope[:, :128])
            slope = jnp.concatenate([seam, slope[:, 128:]], axis=1)
            out_ref[i, j, :, 384:] = slope
            raw[4 * i + j] = raw[4 * i + j] + push(dx[i + 1, j + 1], slope, 384.0)

    first_turn(0, True)
    first_turn(1, True)
    first_turn(0, False)
    first_turn(1, False)
    for made in rounds[0] + rounds[1]:
        when_all(made, 0, "wait_send")
    for n in (0, 1):
        when_all(rounds[2 + n], 1, "wait_recv")
        second_turn(n)
    for made in rounds[2:4]:
        when_all(made, 0, "wait_send")
    when_all(rounds[4], 1, "wait_recv")
    smooth_space(halves[0][16], halves[0][17], halves[0][12])
    lax.fori_loop(0, 4, push_first, 0)
    when_all(rounds[4], 0, "wait_send")
    when_all(rounds[5], 1, "wait_recv")
    smooth_space(halves[1][16], halves[1][17], halves[1][12])
    push_second(0)

    def push_rest(i, carry):
        gather(i - 1)
        push_second(i)
        exchange(i - 1).start()
        return carry

    lax.fori_loop(1, 4, push_rest, 0)
    gather(3)
    exchange(3).start()
    when_all(rounds[5], 0, "wait_send")
    sums.wait_recv()
    weights = wsum[0] + wsum[1]
    for i in range(4):
        exchange(i).wait_recv()
        for j in range(4):
            stacked = (part[0, i, j] + part[1, i, j]) / weights
            for r in range(8):
                stack_ref[i, j:j + 1, 128 * r:128 * r + 128] = stacked[r:r + 1]
    sums.wait_send()
    for i in range(4):
        exchange(i).wait_send()


def moveout(data, offset_weight, counts):
    scratch = []
    for _, width in WINDOWS:
        tiles = pltpu.VMEM((6, 6, 8, width), jnp.float32)
        plane = pltpu.VMEM((6, 8, width), jnp.float32)
        own = pltpu.VMEM((4, 4, 8, width), jnp.float32)
        rows = pltpu.VMEM((4, 8, width), jnp.float32)
        scratch += [tiles, plane, plane, rows, rows, tiles, tiles, plane, plane, tiles, tiles,
                    own, own, own, tiles, plane, tiles, plane,
                    pltpu.VMEM((2, 4, 8, width), jnp.float32), own]
    return pl.pallas_call(
        lambda *refs: moveout_kernel(counts, *refs),
        out_shape=(jax.ShapeDtypeStruct((4, 4, 8, T), jnp.float32),
                   jax.ShapeDtypeStruct((4, 4, T), jnp.float32)),
        in_specs=[pl.BlockSpec(memory_space=pltpu.HBM)] * 2,
        out_specs=(pl.BlockSpec(memory_space=pltpu.VMEM), pl.BlockSpec(memory_space=pltpu.VMEM)),
        scratch_shapes=scratch + [
            pltpu.VMEM((2, 8, 128), jnp.float32),
            pltpu.VMEM((16, 4 * NA, NB), jnp.float32),
            pltpu.VMEM((2, 4, 4, 8, 128), jnp.float32),
            pltpu.SMEM((8,), jnp.float32), pltpu.SemaphoreType.DMA,
            pltpu.SemaphoreType.DMA((2,)), pltpu.SemaphoreType.DMA((6, 27)),
            pltpu.SemaphoreType.DMA((6, 27)), pltpu.SemaphoreType.DMA((2,)),
            pltpu.SemaphoreType.DMA((2, 4))],
        compiler_params=pltpu.CompilerParams(
            collective_id=0, has_side_effects=True, vmem_limit_bytes=48 * 2**20),
        name="moveout",
    )(pltpu.with_memory_space_constraint(offset_weight, pltpu.HBM),
      pltpu.with_memory_space_constraint(data, pltpu.HBM))


def solution(mesh):
    counts = (mesh.shape["il"], mesh.shape["xl"])
    return jax.shard_map(
        lambda data, offset_weight: moveout(data, offset_weight, counts),
        mesh=mesh,
        in_specs=(P("il", "xl", "off", None), P("off")),
        out_specs=(P("il", "xl", "off", None), P("il", "xl", None)),
        check_vma=False,
    )
```

```python
import jax
import jax.numpy as jnp
from jax import lax
from jax.experimental import pallas as pl
from jax.experimental.pallas import tpu as pltpu
from jax.sharding import PartitionSpec as P

T = 1024
NA = 16
NB = 64
damping = 0.05
MESH = pl.DeviceIdType.MESH
STEPS = [(-1, -1), (-1, 1), (1, -1), (1, 1), (0, -1), (0, 1), (0, 0), (-1, 0), (1, 0)]
CENTRE = 9 + STEPS.index((0, 0))
SOURCE = {-1: slice(0, 1), 0: slice(0, 4), 1: slice(3, 4)}
INNER = {-1: slice(1, 2), 0: slice(1, 5), 1: slice(4, 5)}
TARGET = {-1: slice(5, 6), 0: slice(1, 5), 1: slice(0, 1)}
WINDOWS = ((0, 512), (384, 640))
SEAM = 448


def earlier(x, axis):
    x = pltpu.roll(x, 1, axis)
    at = lax.broadcasted_iota(jnp.int32, (8, 128), axis)
    return jnp.concatenate([jnp.where(at == 0, 0.0, x[:, :128]), x[:, 128:]], axis=1)


def later(x, axis):
    n = x.shape[axis]
    x = pltpu.roll(x, n - 1, axis)
    at = lax.broadcasted_iota(jnp.int32, (8, 128), axis)
    return jnp.concatenate([x[:, :n - 128], jnp.where(at == 127, 0.0, x[:, n - 128:])], axis=1)


def smooth_time(u):
    return (earlier(u, 1) + 2.0 * u + later(u, 1)) * (1.0 / 256.0)


def moveout_kernel(counts, weight_hbm, data_hbm, out_ref, stack_ref, *scratch):
    halves, scratch = (scratch[:20], scratch[20:40]), scratch[40:]
    (wsum, raw, part, weight_ref, weight_sem, load_sems, send_sems, recv_sems,
     sum_sems, part_sems, seam_inner) = scratch
    n_il, n_xl = counts
    off, il, xl = lax.axis_index("off"), lax.axis_index("il"), lax.axis_index("xl")
    first = off == 0
    partner = {"off": 1 - off, "il": il, "xl": xl}

    def exists(di, dj):
        i, j = il + di, xl + dj
        return (i >= 0) & (i < n_il) & (j >= 0) & (j < n_xl)

    def transfers(turn, field, planes):
        made = []
        for k, (di, dj) in enumerate(STEPS):
            def copy(slot, to_off, source, target):
                return pltpu.make_async_remote_copy(
                    src_ref=source, dst_ref=target,
                    send_sem=send_sems.at[turn, slot], recv_sem=recv_sems.at[turn, slot],
                    device_id={"off": to_off, "il": il + di, "xl": xl + dj},
                    device_id_type=MESH)
            sends, takes = exists(di, dj), exists(-di, -dj)
            copies = []
            if field is not None and (di, dj) != (0, 0):
                copies.append(copy(k, off, field.at[INNER[di], INNER[dj]],
                                   field.at[TARGET[di], TARGET[dj]]))
            for n, (source, target) in enumerate(planes):
                plane = copy(9 + 9 * n + k, 1 - off, source.at[SOURCE[di], SOURCE[dj]],
                             target.at[TARGET[di], TARGET[dj]])
                if n == 0:
                    copies.append(plane)
                else:
                    made.append((sends & (off == 1), takes & first, [plane], 18 + k))
            if copies:
                made.append((sends, takes, copies, 9 + k))
        return made

    def when_all(made, which, act):
        for item in made:
            @pl.when(item[which])
            def _():
                for copy in item[2]:
                    getattr(copy, act)()

    loads = []
    for n, (base, width) in enumerate(WINDOWS):
        load = pltpu.make_async_copy(
            data_hbm.at[:, :, :, base:base + width], halves[n][0].at[1:5, 1:5], load_sems.at[n])
        load.start()
        loads.append(load)
    load_weight = pltpu.make_async_copy(weight_hbm, weight_ref, weight_sem)
    load_weight.start()
    barrier = pltpu.get_barrier_semaphore()
    for di, dj in STEPS:
        for o in (0, 1):
            if (di, dj, o) != (0, 0, 0):
                @pl.when(exists(di, dj))
                def _():
                    pl.semaphore_signal(
                        barrier, inc=1, device_id_type=MESH,
                        device_id={"off": (off + o) % 2, "il": il + di, "xl": xl + dj})
    rows_near = 1 + (il > 0).astype(jnp.int32) + (il < n_il - 1).astype(jnp.int32)
    cols_near = 1 + (xl > 0).astype(jnp.int32) + (xl < n_xl - 1).astype(jnp.int32)

    load_weight.wait()
    total = weight_ref[0]
    for h in range(1, 8):
        total = total + weight_ref[h]
    wsum[0] = jnp.full((8, 128), total, jnp.float32)
    for load in loads:
        load.wait()
    pl.semaphore_wait(barrier, 2 * rows_near * cols_near - 1)

    rounds = []
    for n, half in enumerate(halves):
        dx, d0, d1, p0, p1 = half[:5]
        made = transfers(n, dx, [])
        when_all(made, 0, "start")
        for i in range(4):
            for j in range(4):
                tile = dx[1 + i, 1 + j]
                p0[i, j:j + 1] = jnp.where(first, tile[7:8], tile[0:1])
                p1[i, j:j + 1] = tile[1:2]
        plane = transfers(n, None, [(p0, d0), (p1, d1)])
        when_all(plane, 0, "start")
        rounds.append((made, plane))
    sums = pltpu.make_async_remote_copy(
        src_ref=wsum.at[0], dst_ref=wsum.at[1], send_sem=sum_sems.at[0], recv_sem=sum_sems.at[1],
        device_id=partner, device_id_type=MESH)
    sums.start()

    for di, dj in STEPS:
        if (di, dj) != (0, 0):
            @pl.when(jnp.logical_not(exists(-di, -dj)))
            def _():
                for half in halves:
                    for n in (0, 1, 2, 14, 15, 16, 17):
                        shape = half[n].at[TARGET[di], TARGET[dj]].shape
                        half[n][TARGET[di], TARGET[dj]] = jnp.zeros(shape, jnp.float32)

    keep_next = jnp.where(first, 1.0, 0.0)
    keep_before = 1.0 - keep_next
    row = lax.broadcasted_iota(jnp.int32, (8, 128), 0)
    lane = lax.broadcasted_iota(jnp.int32, (8, 128), 1)

    def smooth_space(field, plane, out):
        def column(c, carry):
            lanes = pl.ds(pl.multiple_of(c * 128, 128), 128)
            sums_xl = []
            for i in range(6):
                tiles = [field[i, j, :, lanes] for j in range(6)]
                pairs = [tiles[j] + tiles[j + 1] for j in range(5)]
                sums_xl.append([pairs[j] + pairs[j + 1] for j in range(4)])
            halo = [plane[i, :, lanes] for i in range(6)]
            for i in range(4):
                h = halo[i] + 2.0 * halo[i + 1] + halo[i + 2]
                h = pltpu.roll(h, 1, 0) + 2.0 * h + pltpu.roll(h, 7, 0)
                before = h * keep_before
                after = h * keep_next
                for j in range(4):
                    x = sums_xl[i][j] + 2.0 * sums_xl[i + 1][j] + sums_xl[i + 2][j]
                    up = jnp.broadcast_to(before[j + 1:j + 2], (8, 128))
                    down = jnp.broadcast_to(after[j + 1:j + 2], (8, 128))
                    up = jnp.where(row == 0, up, pltpu.roll(x, 1, 0))
                    down = jnp.where(row == 7, down, pltpu.roll(x, 7, 0))
                    out[i, j, :, lanes] = up + 2.0 * x + down
            return carry
        lax.fori_loop(0, field.shape[3] // 128, column, 0)

    def smooth_inner(field, out):
        def column(c, carry):
            lanes = pl.ds(pl.multiple_of(c * 128, 128), 128)
            sums_xl = []
            for i in range(1, 5):
                tiles = [field[i, j, :, lanes] for j in range(1, 5)]
                pairs = [tiles[j] + tiles[j + 1] for j in range(3)]
                sums_xl.append([pairs[j] + pairs[j + 1] for j in range(2)])
            for i in range(2):
                for j in range(2):
                    x = sums_xl[i][j] + 2.0 * sums_xl[i + 1][j] + sums_xl[i + 2][j]
                    up = jnp.where(row == 0, 0.0, pltpu.roll(x, 1, 0))
                    down = jnp.where(row == 7, 0.0, pltpu.roll(x, 7, 0))
                    out[1 + i, 1 + j, :, lanes] = up + 2.0 * x + down
            return carry
        lax.fori_loop(0, field.shape[3] // 128, column, 0)

    def first_turn(n, inner):
        dx, d0, d1, _, _, gg, gr, hgg, hgr, grad, res, rden, ub, uc, q2, o2, q3, o3, pq, own = \
            halves[n]
        width = WINDOWS[n][1]
        row8 = lax.broadcasted_iota(jnp.int32, (8, width), 0)

        def gradients(i, j):
            d = dx[i, j]
            edge = jnp.broadcast_to(d0[i, j:j + 1] * keep_next, (8, width))
            f = jnp.where(row8 == 7, edge, pltpu.roll(d, 7, 0))
            r = f - d
            s = d + f
            g = 0.25 * (later(s, 1) - earlier(s, 1))
            gg[i, j] = g * g
            gr[i, j] = g * r
            grad[i, j] = g
            res[i, j] = r

        made, plane = rounds[n]
        if inner:
            centre = [item for item in plane if item[3] == CENTRE]
            when_all(centre, 1, "wait_recv")
            for i in range(1, 5):
                for j in range(1, 5):
                    gradients(i, j)
            return
        when_all(made + [item for item in plane if item[3] != CENTRE], 1, "wait_recv")

        @pl.when(off == 1)
        def _():
            for i in range(6):
                for j in range(6):
                    d1[i, j:j + 1] = dx[i, j, 0:1]

        for i in range(6):
            for j in range(6):
                if i in (0, 5) or j in (0, 5):
                    gradients(i, j)
            d, f = d0[i], d1[i]
            s = d + f
            g = 0.25 * (later(s, 1) - earlier(s, 1))
            hgg[i] = g * g
            hgr[i] = g * (f - d)

        smooth_space(gg, hgg, ub)
        smooth_space(gr, hgr, uc)

        def start_slope(i, carry):
            for j in range(4):
                inverse = 1.0 / (smooth_time(ub[i, j]) + damping)
                rden[i, j] = inverse
                slope = -smooth_time(uc[i, j]) * inverse
                own[i, j] = slope
                g = grad[i + 1, j + 1]
                q = g * (res[i + 1, j + 1] + slope * g)
                q2[i + 1, j + 1] = q
                pq[0, i, j:j + 1] = jnp.where(first, q[7:8], q[0:1])
            return carry

        lax.fori_loop(0, 4, start_slope, 0, unroll=2)
        made = transfers(2 + n, q2, [(pq.at[0], o2)])
        when_all(made, 0, "start")
        rounds.append(made)

    def second_turn(n):
        grad, res, rden, ub, q2, o2, q3, pq, own = (halves[n][k] for k in (
            9, 10, 11, 12, 14, 15, 16, 18, 19))
        smooth_space(q2, o2, ub)

        def next_slope(i, carry):
            for j in range(4):
                slope = own[i, j] - smooth_time(ub[i, j]) * rden[i, j]
                own[i, j] = slope
                g = grad[i + 1, j + 1]
                q = g * (res[i + 1, j + 1] + slope * g)
                q3[i + 1, j + 1] = q
                pq[1, i, j:j + 1] = jnp.where(first, q[7:8], q[0:1])
            return carry

        lax.fori_loop(0, 4, next_slope, 0, unroll=4)
        made = transfers(4 + n, q3, [(pq.at[1], halves[n][17])])
        when_all(made, 0, "start")
        rounds.append(made)

    weight = jnp.full((8, 128), weight_ref[0], jnp.float32)
    for h in range(1, 8):
        weight = jnp.where(row == h, weight_ref[h], weight)
    edge_row = jnp.where(first, 7, 0)
    inner_weight = jnp.where(row == edge_row, 0.0, weight)
    high = lax.broadcasted_iota(jnp.int32, (NA, 128), 0)
    high = jnp.where(high < 8, 2 * high, 2 * high - 15)
    high = high.astype(jnp.float32).astype(jnp.bfloat16)
    low = lax.broadcasted_iota(jnp.int32, (NB, 128), 0).astype(jnp.float32).astype(jnp.bfloat16)
    zero_a = jnp.zeros((NA, 128), jnp.bfloat16)
    zero_b = jnp.zeros((NB, 128), jnp.bfloat16)
    one_b = jnp.ones((NB, 128), jnp.bfloat16)

    def push(data, slope, start, kind="full"):
        width = data.shape[1]
        tt = lax.broadcasted_iota(jnp.int32, (8, width), 1).astype(jnp.float32) + (start + 1.0)
        hh = lax.broadcasted_iota(jnp.int32, (8, width), 0).astype(jnp.float32) + 0.5
        hh = hh + 8.0 * keep_before
        place = jnp.sqrt(jnp.maximum(tt * tt - tt * hh * slope, 1.0)) - 1.0
        cell = jnp.floor(place)
        f = place - cell
        cell = jnp.minimum(cell, float(T))
        a = jnp.floor(cell * (1.0 / NB))
        b = cell - a * NB
        scale = inner_weight if kind == "inner" else weight
        v = data * jnp.concatenate([scale] * (width // 128), axis=1)
        x1 = v * f
        x0 = v - x1
        x0h = x0.astype(jnp.bfloat16).astype(jnp.float32)
        x1h = x1.astype(jnp.bfloat16).astype(jnp.float32)
        values = (x0h, x0 - x0h, x1h, x1 - x1h)
        groups = [(h, h + 1) for h in range(0, 8, 2)]
        if kind == "edge":
            a, b, *values = [jnp.where(first, x[7:8], x[0:1]) for x in (a, b) + values]
            groups = [(0,)]
        acc = jnp.zeros((4 * NA, NB), jnp.float32)
        for group in groups:
            left, right = [], []
            for k in group:
                for c in range(0, width, 128):
                    def spread(x, n):
                        piece = x[k:k + 1, c:c + 128]
                        return jnp.broadcast_to(piece, (n, 128)).astype(jnp.bfloat16)
                    hit = spread(a, NA) == high
                    left.append(jnp.concatenate(
                        [jnp.where(hit, spread(x, NA), zero_a) for x in values], axis=0))
                    right.append(jnp.where(spread(b, NB) == low, one_b, zero_b))
            dot = lax.dot_general(
                jnp.concatenate(left, axis=1), jnp.concatenate(right, axis=1),
                (((1,), (1,)), ((), ())), preferred_element_type=jnp.float32)
            acc = acc + jnp.maximum(dot, -3.0e38)
        return acc

    def gather(i):
        for j in range(4):
            acc = raw[4 * i + j]
            lower = acc[:NA] + acc[NA:2 * NA]
            upper = acc[2 * NA:3 * NA] + acc[3 * NA:]
            lower = jnp.concatenate([lower[:8], lower[8:]], axis=1)
            upper = jnp.concatenate([upper[:8], upper[8:]], axis=1)
            upper = pltpu.roll(upper, 1, 1)
            before = pltpu.roll(upper, 1, 0)
            upper = jnp.where(lane == 0, jnp.where(row == 0, 0.0, before), upper)
            part[0, i, j] = lower + upper

    def exchange(i):
        return pltpu.make_async_remote_copy(
            src_ref=part.at[0, i], dst_ref=part.at[1, i],
            send_sem=part_sems.at[0, i], recv_sem=part_sems.at[1, i],
            device_id=partner, device_id_type=MESH)

    def last_slope(n, i, j):
        rden, ub, own = (halves[n][k] for k in (11, 12, 19))
        return own[i, j] - smooth_time(ub[i, j]) * rden[i, j]

    def push_first(i, j, kind):
        slope = last_slope(0, i, j)
        added = push(halves[0][0][i + 1, j + 1, :, :384], slope[:, :384], 0.0, kind)
        if kind == "inner":
            seam_inner[i - 1, j - 1] = slope[:, 384:]
        else:
            halves[0][19][i, j] = slope
            out_ref[i, j, :, :384] = slope[:, :384]
        if kind == "edge":
            added = raw[4 * i + j] + added
        raw[4 * i + j] = added

    def push_second(i, j, kind):
        slope = last_slope(1, i, j)
        before = seam_inner[i - 1, j - 1] if kind == "inner" else halves[0][19][i, j, :, 384:]
        seam = jnp.where(lane < SEAM - 384, before, slope[:, :128])
        slope = jnp.concatenate([seam, slope[:, 128:]], axis=1)
        if kind != "inner":
            out_ref[i, j, :, 384:] = slope
        added = push(halves[1][0][i + 1, j + 1], slope, 384.0, kind)
        raw[4 * i + j] = raw[4 * i + j] + added

    inner = [(i, j) for i in (1, 2) for j in (1, 2)]
    sides = [(i, j) for i in (1, 2) for j in (0, 3)]

    for n in (0, 1):
        first_turn(n, True)
        first_turn(n, False)
    for made in rounds[0] + rounds[1]:
        when_all(made, 0, "wait_send")
    for n in (0, 1):
        when_all(rounds[2 + n], 1, "wait_recv")
        second_turn(n)
    smooth_inner(halves[0][16], halves[0][12])
    for i, j in inner:
        push_first(i, j, "inner")
    smooth_inner(halves[1][16], halves[1][12])
    for i, j in inner:
        push_second(i, j, "inner")
    for made in rounds[2:4]:
        when_all(made, 0, "wait_send")

    when_all(rounds[4], 1, "wait_recv")
    smooth_space(halves[0][16], halves[0][17], halves[0][12])

    def push_row(k, carry):
        for j in range(4):
            push_first(3 * k, j, "full")
        return carry

    lax.fori_loop(0, 2, push_row, 0)
    for i, j in sides:
        push_first(i, j, "full")
    for i, j in inner:
        push_first(i, j, "edge")
    when_all(rounds[4], 0, "wait_send")
    when_all(rounds[5], 1, "wait_recv")
    smooth_space(halves[1][16], halves[1][17], halves[1][12])
    for j in range(4):
        push_second(0, j, "full")
    gather(0)
    for i, j in sides:
        push_second(i, j, "full")
    for i, j in inner:
        push_second(i, j, "edge")
    exchange(0).start()
    gather(1)
    gather(2)
    for j in range(4):
        push_second(3, j, "full")
    exchange(1).start()
    exchange(2).start()
    gather(3)
    exchange(3).start()
    when_all(rounds[5], 0, "wait_send")
    sums.wait_recv()
    weights = wsum[0] + wsum[1]
    for i in range(4):
        exchange(i).wait_recv()
        for j in range(4):
            stacked = (part[0, i, j] + part[1, i, j]) / weights
            for r in range(8):
                stack_ref[i, j:j + 1, 128 * r:128 * r + 128] = stacked[r:r + 1]
    sums.wait_send()
    for i in range(4):
        exchange(i).wait_send()


def moveout(data, offset_weight, counts):
    scratch = []
    for _, width in WINDOWS:
        tiles = pltpu.VMEM((6, 6, 8, width), jnp.float32)
        plane = pltpu.VMEM((6, 8, width), jnp.float32)
        own = pltpu.VMEM((4, 4, 8, width), jnp.float32)
        rows = pltpu.VMEM((4, 8, width), jnp.float32)
        scratch += [tiles, plane, plane, rows, rows, tiles, tiles, plane, plane, tiles, tiles,
                    own, own, own, tiles, plane, tiles, plane,
                    pltpu.VMEM((2, 4, 8, width), jnp.float32), own]
    return pl.pallas_call(
        lambda *refs: moveout_kernel(counts, *refs),
        out_shape=(jax.ShapeDtypeStruct((4, 4, 8, T), jnp.float32),
                   jax.ShapeDtypeStruct((4, 4, T), jnp.float32)),
        in_specs=[pl.BlockSpec(memory_space=pltpu.HBM)] * 2,
        out_specs=(pl.BlockSpec(memory_space=pltpu.VMEM), pl.BlockSpec(memory_space=pltpu.VMEM)),
        scratch_shapes=scratch + [
            pltpu.VMEM((2, 8, 128), jnp.float32),
            pltpu.VMEM((16, 4 * NA, NB), jnp.float32),
            pltpu.VMEM((2, 4, 4, 8, 128), jnp.float32),
            pltpu.SMEM((8,), jnp.float32), pltpu.SemaphoreType.DMA,
            pltpu.SemaphoreType.DMA((2,)), pltpu.SemaphoreType.DMA((6, 27)),
            pltpu.SemaphoreType.DMA((6, 27)), pltpu.SemaphoreType.DMA((2,)),
            pltpu.SemaphoreType.DMA((2, 4)), pltpu.VMEM((2, 2, 8, 128), jnp.float32)],
        compiler_params=pltpu.CompilerParams(
            collective_id=0, has_side_effects=True, vmem_limit_bytes=48 * 2**20),
        name="moveout",
    )(pltpu.with_memory_space_constraint(offset_weight, pltpu.HBM),
      pltpu.with_memory_space_constraint(data, pltpu.HBM))


def solution(mesh):
    counts = (mesh.shape["il"], mesh.shape["xl"])
    return jax.shard_map(
        lambda data, offset_weight: moveout(data, offset_weight, counts),
        mesh=mesh,
        in_specs=(P("il", "xl", "off", None), P("off")),
        out_specs=(P("il", "xl", "off", None), P("il", "xl", None)),
        check_vma=False,
    )
```

```python
import jax
import jax.numpy as jnp
from jax import lax
from jax.experimental import pallas as pl
from jax.experimental.pallas import tpu as pltpu
from jax.sharding import PartitionSpec as P

T = 1024
NA = 16
NB = 64
damping = 0.05
MESH = pl.DeviceIdType.MESH
STEPS = [(-1, -1), (-1, 1), (1, -1), (1, 1), (0, -1), (0, 1), (0, 0), (-1, 0), (1, 0)]
CENTRE = 9 + STEPS.index((0, 0))
SOURCE = {-1: slice(0, 1), 0: slice(0, 4), 1: slice(3, 4)}
INNER = {-1: slice(1, 2), 0: slice(1, 5), 1: slice(4, 5)}
TARGET = {-1: slice(5, 6), 0: slice(1, 5), 1: slice(0, 1)}
WINDOWS = ((0, 512), (384, 640))
SEAM = 448


def earlier(x, axis):
    x = pltpu.roll(x, 1, axis)
    at = lax.broadcasted_iota(jnp.int32, (8, 128), axis)
    return jnp.concatenate([jnp.where(at == 0, 0.0, x[:, :128]), x[:, 128:]], axis=1)


def later(x, axis):
    n = x.shape[axis]
    x = pltpu.roll(x, n - 1, axis)
    at = lax.broadcasted_iota(jnp.int32, (8, 128), axis)
    return jnp.concatenate([x[:, :n - 128], jnp.where(at == 127, 0.0, x[:, n - 128:])], axis=1)


def smooth_time(u):
    return (earlier(u, 1) + 2.0 * u + later(u, 1)) * (1.0 / 256.0)


def moveout_kernel(counts, weight_hbm, data_hbm, out_ref, stack_ref, *scratch):
    halves, scratch = (scratch[:20], scratch[20:40]), scratch[40:]
    (wsum, raw, part, weight_ref, weight_sem, load_sems, send_sems, recv_sems,
     sum_sems, part_sems, seam_inner) = scratch
    n_il, n_xl = counts
    off, il, xl = lax.axis_index("off"), lax.axis_index("il"), lax.axis_index("xl")
    first = off == 0
    partner = {"off": 1 - off, "il": il, "xl": xl}

    def exists(di, dj):
        i, j = il + di, xl + dj
        return (i >= 0) & (i < n_il) & (j >= 0) & (j < n_xl)

    def transfers(turn, field, planes):
        made = []
        for k, (di, dj) in enumerate(STEPS):
            def copy(slot, to_off, source, target):
                return pltpu.make_async_remote_copy(
                    src_ref=source, dst_ref=target,
                    send_sem=send_sems.at[turn, slot], recv_sem=recv_sems.at[turn, slot],
                    device_id={"off": to_off, "il": il + di, "xl": xl + dj},
                    device_id_type=MESH)
            sends, takes = exists(di, dj), exists(-di, -dj)
            copies = []
            if field is not None and (di, dj) != (0, 0):
                copies.append(copy(k, off, field.at[INNER[di], INNER[dj]],
                                   field.at[TARGET[di], TARGET[dj]]))
            for n, (source, target) in enumerate(planes):
                plane = copy(9 + 9 * n + k, 1 - off, source.at[SOURCE[di], SOURCE[dj]],
                             target.at[TARGET[di], TARGET[dj]])
                if n == 0:
                    copies.append(plane)
                else:
                    made.append((sends & (off == 1), takes & first, [plane], 18 + k))
            if copies:
                made.append((sends, takes, copies, 9 + k))
        return made

    def when_all(made, which, act):
        for item in made:
            @pl.when(item[which])
            def _():
                for copy in item[2]:
                    getattr(copy, act)()

    loads = []
    for n, (base, width) in enumerate(WINDOWS):
        load = pltpu.make_async_copy(
            data_hbm.at[:, :, :, base:base + width], halves[n][0].at[1:5, 1:5], load_sems.at[n])
        load.start()
        loads.append(load)
    load_weight = pltpu.make_async_copy(weight_hbm, weight_ref, weight_sem)
    load_weight.start()
    barrier = pltpu.get_barrier_semaphore()
    for di, dj in STEPS:
        for o in (0, 1):
            if (di, dj, o) != (0, 0, 0):
                @pl.when(exists(di, dj))
                def _():
                    pl.semaphore_signal(
                        barrier, inc=1, device_id_type=MESH,
                        device_id={"off": (off + o) % 2, "il": il + di, "xl": xl + dj})
    rows_near = 1 + (il > 0).astype(jnp.int32) + (il < n_il - 1).astype(jnp.int32)
    cols_near = 1 + (xl > 0).astype(jnp.int32) + (xl < n_xl - 1).astype(jnp.int32)

    load_weight.wait()
    total = weight_ref[0]
    for h in range(1, 8):
        total = total + weight_ref[h]
    wsum[0] = jnp.full((8, 128), total, jnp.float32)
    for load in loads:
        load.wait()
    pl.semaphore_wait(barrier, 2 * rows_near * cols_near - 1)

    rounds = []
    for n, half in enumerate(halves):
        dx, d0, d1, p0, p1 = half[:5]
        made = transfers(n, dx, [])
        when_all(made, 0, "start")
        for i in range(4):
            for j in range(4):
                tile = dx[1 + i, 1 + j]
                p0[i, j:j + 1] = jnp.where(first, tile[7:8], tile[0:1])
                p1[i, j:j + 1] = tile[1:2]
        plane = transfers(n, None, [(p0, d0), (p1, d1)])
        when_all(plane, 0, "start")
        rounds.append((made, plane))
    sums = pltpu.make_async_remote_copy(
        src_ref=wsum.at[0], dst_ref=wsum.at[1], send_sem=sum_sems.at[0], recv_sem=sum_sems.at[1],
        device_id=partner, device_id_type=MESH)
    sums.start()

    for di, dj in STEPS:
        if (di, dj) != (0, 0):
            @pl.when(jnp.logical_not(exists(-di, -dj)))
            def _():
                for half in halves:
                    for n in (0, 1, 2, 14, 15, 16, 17):
                        shape = half[n].at[TARGET[di], TARGET[dj]].shape
                        half[n][TARGET[di], TARGET[dj]] = jnp.zeros(shape, jnp.float32)

    keep_next = jnp.where(first, 1.0, 0.0)
    keep_before = 1.0 - keep_next
    row = lax.broadcasted_iota(jnp.int32, (8, 128), 0)
    lane = lax.broadcasted_iota(jnp.int32, (8, 128), 1)

    def smooth_space(field, plane, out):
        def column(c, carry):
            lanes = pl.ds(pl.multiple_of(c * 128, 128), 128)
            sums_xl = []
            for i in range(6):
                tiles = [field[i, j, :, lanes] for j in range(6)]
                pairs = [tiles[j] + tiles[j + 1] for j in range(5)]
                sums_xl.append([pairs[j] + pairs[j + 1] for j in range(4)])
            halo = [plane[i, :, lanes] for i in range(6)]
            for i in range(4):
                h = halo[i] + 2.0 * halo[i + 1] + halo[i + 2]
                h = pltpu.roll(h, 1, 0) + 2.0 * h + pltpu.roll(h, 7, 0)
                before = h * keep_before
                after = h * keep_next
                for j in range(4):
                    x = sums_xl[i][j] + 2.0 * sums_xl[i + 1][j] + sums_xl[i + 2][j]
                    up = jnp.broadcast_to(before[j + 1:j + 2], (8, 128))
                    down = jnp.broadcast_to(after[j + 1:j + 2], (8, 128))
                    up = jnp.where(row == 0, up, pltpu.roll(x, 1, 0))
                    down = jnp.where(row == 7, down, pltpu.roll(x, 7, 0))
                    out[i, j, :, lanes] = up + 2.0 * x + down
            return carry
        lax.fori_loop(0, field.shape[3] // 128, column, 0, unroll=True)

    def smooth_inner(field, out):
        def column(c, carry):
            lanes = pl.ds(pl.multiple_of(c * 128, 128), 128)
            sums_xl = []
            for i in range(1, 5):
                tiles = [field[i, j, :, lanes] for j in range(1, 5)]
                pairs = [tiles[j] + tiles[j + 1] for j in range(3)]
                sums_xl.append([pairs[j] + pairs[j + 1] for j in range(2)])
            for i in range(2):
                for j in range(2):
                    x = sums_xl[i][j] + 2.0 * sums_xl[i + 1][j] + sums_xl[i + 2][j]
                    up = jnp.where(row == 0, 0.0, pltpu.roll(x, 1, 0))
                    down = jnp.where(row == 7, 0.0, pltpu.roll(x, 7, 0))
                    out[1 + i, 1 + j, :, lanes] = up + 2.0 * x + down
            return carry
        lax.fori_loop(0, field.shape[3] // 128, column, 0, unroll=True)

    def first_turn(n, inner):
        dx, d0, d1, _, _, gg, gr, hgg, hgr, grad, res, rden, ub, uc, q2, o2, q3, o3, pq, own = \
            halves[n]
        width = WINDOWS[n][1]
        row8 = lax.broadcasted_iota(jnp.int32, (8, width), 0)

        def gradients(i, j):
            d = dx[i, j]
            edge = jnp.broadcast_to(d0[i, j:j + 1] * keep_next, (8, width))
            f = jnp.where(row8 == 7, edge, pltpu.roll(d, 7, 0))
            r = f - d
            s = d + f
            g = 0.25 * (later(s, 1) - earlier(s, 1))
            gg[i, j] = g * g
            gr[i, j] = g * r
            grad[i, j] = g
            res[i, j] = r

        made, plane = rounds[n]
        if inner:
            centre = [item for item in plane if item[3] == CENTRE]
            when_all(centre, 1, "wait_recv")
            for i in range(1, 5):
                for j in range(1, 5):
                    gradients(i, j)
            return
        when_all(made + [item for item in plane if item[3] != CENTRE], 1, "wait_recv")

        @pl.when(off == 1)
        def _():
            for i in range(6):
                for j in range(6):
                    d1[i, j:j + 1] = dx[i, j, 0:1]

        for i in range(6):
            for j in range(6):
                if i in (0, 5) or j in (0, 5):
                    gradients(i, j)
            d, f = d0[i], d1[i]
            s = d + f
            g = 0.25 * (later(s, 1) - earlier(s, 1))
            hgg[i] = g * g
            hgr[i] = g * (f - d)

        smooth_space(gg, hgg, ub)
        smooth_space(gr, hgr, uc)

        def start_slope(i, carry):
            for j in range(4):
                inverse = 1.0 / (smooth_time(ub[i, j]) + damping)
                rden[i, j] = inverse
                slope = -smooth_time(uc[i, j]) * inverse
                own[i, j] = slope
                g = grad[i + 1, j + 1]
                q = g * (res[i + 1, j + 1] + slope * g)
                q2[i + 1, j + 1] = q
                pq[0, i, j:j + 1] = jnp.where(first, q[7:8], q[0:1])
            return carry

        lax.fori_loop(0, 4, start_slope, 0, unroll=True)
        made = transfers(2 + n, q2, [(pq.at[0], o2)])
        when_all(made, 0, "start")
        rounds.append(made)

    def second_turn(n):
        grad, res, rden, ub, q2, o2, q3, pq, own = (halves[n][k] for k in (
            9, 10, 11, 12, 14, 15, 16, 18, 19))
        smooth_space(q2, o2, ub)

        def next_slope(i, carry):
            for j in range(4):
                slope = own[i, j] - smooth_time(ub[i, j]) * rden[i, j]
                own[i, j] = slope
                g = grad[i + 1, j + 1]
                q = g * (res[i + 1, j + 1] + slope * g)
                q3[i + 1, j + 1] = q
                pq[1, i, j:j + 1] = jnp.where(first, q[7:8], q[0:1])
            return carry

        lax.fori_loop(0, 4, next_slope, 0, unroll=4)
        made = transfers(4 + n, q3, [(pq.at[1], halves[n][17])])
        when_all(made, 0, "start")
        rounds.append(made)

    weight = jnp.full((8, 128), weight_ref[0], jnp.float32)
    for h in range(1, 8):
        weight = jnp.where(row == h, weight_ref[h], weight)
    edge_row = jnp.where(first, 7, 0)
    inner_weight = jnp.where(row == edge_row, 0.0, weight)
    high = lax.broadcasted_iota(jnp.int32, (NA, 128), 0)
    high = jnp.where(high < 8, 2 * high, 2 * high - 15)
    high = high.astype(jnp.float32).astype(jnp.bfloat16)
    low = lax.broadcasted_iota(jnp.int32, (NB, 128), 0).astype(jnp.float32).astype(jnp.bfloat16)
    zero_a = jnp.zeros((NA, 128), jnp.bfloat16)
    zero_b = jnp.zeros((NB, 128), jnp.bfloat16)
    one_b = jnp.ones((NB, 128), jnp.bfloat16)

    def push(data, slope, start, kind="full"):
        width = data.shape[1]
        tt = lax.broadcasted_iota(jnp.int32, (8, width), 1).astype(jnp.float32) + (start + 1.0)
        hh = lax.broadcasted_iota(jnp.int32, (8, width), 0).astype(jnp.float32) + 0.5
        hh = hh + 8.0 * keep_before
        place = jnp.sqrt(jnp.maximum(tt * tt - tt * hh * slope, 1.0)) - 1.0
        cell = jnp.floor(place)
        f = place - cell
        cell = jnp.minimum(cell, float(T))
        a = jnp.floor(cell * (1.0 / NB))
        b = cell - a * NB
        scale = inner_weight if kind == "inner" else weight
        v = data * jnp.concatenate([scale] * (width // 128), axis=1)
        x1 = v * f
        x0 = v - x1
        x0h = x0.astype(jnp.bfloat16).astype(jnp.float32)
        x1h = x1.astype(jnp.bfloat16).astype(jnp.float32)
        values = (x0h, x0 - x0h, x1h, x1 - x1h)
        groups = [(h, h + 1) for h in range(0, 8, 2)]
        if kind == "edge":
            a, b, *values = [jnp.where(first, x[7:8], x[0:1]) for x in (a, b) + values]
            groups = [(0,)]
        acc = jnp.zeros((4 * NA, NB), jnp.float32)
        for group in groups:
            left, right = [], []
            for k in group:
                for c in range(0, width, 128):
                    def spread(x, n):
                        piece = x[k:k + 1, c:c + 128]
                        return jnp.broadcast_to(piece, (n, 128)).astype(jnp.bfloat16)
                    hit = spread(a, NA) == high
                    left.append(jnp.concatenate(
                        [jnp.where(hit, spread(x, NA), zero_a) for x in values], axis=0))
                    right.append(jnp.where(spread(b, NB) == low, one_b, zero_b))
            dot = lax.dot_general(
                jnp.concatenate(left, axis=1), jnp.concatenate(right, axis=1),
                (((1,), (1,)), ((), ())), preferred_element_type=jnp.float32)
            acc = acc + jnp.maximum(dot, -3.0e38)
        return acc

    def gather(i):
        for j in range(4):
            acc = raw[4 * i + j]
            lower = acc[:NA] + acc[NA:2 * NA]
            upper = acc[2 * NA:3 * NA] + acc[3 * NA:]
            lower = jnp.concatenate([lower[:8], lower[8:]], axis=1)
            upper = jnp.concatenate([upper[:8], upper[8:]], axis=1)
            upper = pltpu.roll(upper, 1, 1)
            before = pltpu.roll(upper, 1, 0)
            upper = jnp.where(lane == 0, jnp.where(row == 0, 0.0, before), upper)
            part[0, i, j] = lower + upper

    def exchange(i):
        return pltpu.make_async_remote_copy(
            src_ref=part.at[0, i], dst_ref=part.at[1, i],
            send_sem=part_sems.at[0, i], recv_sem=part_sems.at[1, i],
            device_id=partner, device_id_type=MESH)

    def last_slope(n, i, j):
        rden, ub, own = (halves[n][k] for k in (11, 12, 19))
        return own[i, j] - smooth_time(ub[i, j]) * rden[i, j]

    def push_first(i, j, kind):
        slope = last_slope(0, i, j)
        added = push(halves[0][0][i + 1, j + 1, :, :384], slope[:, :384], 0.0, kind)
        if kind == "inner":
            seam_inner[i - 1, j - 1] = slope[:, 384:]
        else:
            halves[0][19][i, j] = slope
            out_ref[i, j, :, :384] = slope[:, :384]
        if kind == "edge":
            added = raw[4 * i + j] + added
        raw[4 * i + j] = added

    def push_second(i, j, kind):
        slope = last_slope(1, i, j)
        before = seam_inner[i - 1, j - 1] if kind == "inner" else halves[0][19][i, j, :, 384:]
        seam = jnp.where(lane < SEAM - 384, before, slope[:, :128])
        slope = jnp.concatenate([seam, slope[:, 128:]], axis=1)
        if kind != "inner":
            out_ref[i, j, :, 384:] = slope
        added = push(halves[1][0][i + 1, j + 1], slope, 384.0, kind)
        raw[4 * i + j] = raw[4 * i + j] + added

    inner = [(i, j) for i in (1, 2) for j in (1, 2)]
    sides = [(i, j) for i in (1, 2) for j in (0, 3)]

    for n in (0, 1):
        first_turn(n, True)
        first_turn(n, False)
    for made in rounds[0] + rounds[1]:
        when_all(made, 0, "wait_send")
    for n in (0, 1):
        when_all(rounds[2 + n], 1, "wait_recv")
        second_turn(n)
    smooth_inner(halves[0][16], halves[0][12])
    for i, j in inner:
        push_first(i, j, "inner")
    smooth_inner(halves[1][16], halves[1][12])
    for i, j in inner:
        push_second(i, j, "inner")
    for made in rounds[2:4]:
        when_all(made, 0, "wait_send")

    when_all(rounds[4], 1, "wait_recv")
    smooth_space(halves[0][16], halves[0][17], halves[0][12])

    def push_row(k, carry):
        for j in range(4):
            push_first(3 * k, j, "full")
        return carry

    lax.fori_loop(0, 2, push_row, 0)
    for i, j in sides:
        push_first(i, j, "full")
    for i, j in inner:
        push_first(i, j, "edge")
    when_all(rounds[4], 0, "wait_send")
    when_all(rounds[5], 1, "wait_recv")
    smooth_space(halves[1][16], halves[1][17], halves[1][12])
    for j in range(4):
        push_second(0, j, "full")
    gather(0)
    for i, j in sides:
        push_second(i, j, "full")
    for i, j in inner:
        push_second(i, j, "edge")
    exchange(0).start()
    gather(1)
    gather(2)
    for j in range(4):
        push_second(3, j, "full")
    exchange(1).start()
    exchange(2).start()
    gather(3)
    exchange(3).start()
    when_all(rounds[5], 0, "wait_send")
    sums.wait_recv()
    weights = wsum[0] + wsum[1]
    for i in range(4):
        exchange(i).wait_recv()
        for j in range(4):
            stacked = (part[0, i, j] + part[1, i, j]) / weights
            for r in range(8):
                stack_ref[i, j:j + 1, 128 * r:128 * r + 128] = stacked[r:r + 1]
    sums.wait_send()
    for i in range(4):
        exchange(i).wait_send()


def moveout(data, offset_weight, counts):
    scratch = []
    for _, width in WINDOWS:
        tiles = pltpu.VMEM((6, 6, 8, width), jnp.float32)
        plane = pltpu.VMEM((6, 8, width), jnp.float32)
        own = pltpu.VMEM((4, 4, 8, width), jnp.float32)
        rows = pltpu.VMEM((4, 8, width), jnp.float32)
        scratch += [tiles, plane, plane, rows, rows, tiles, tiles, plane, plane, tiles, tiles,
                    own, own, own, tiles, plane, tiles, plane,
                    pltpu.VMEM((2, 4, 8, width), jnp.float32), own]
    return pl.pallas_call(
        lambda *refs: moveout_kernel(counts, *refs),
        out_shape=(jax.ShapeDtypeStruct((4, 4, 8, T), jnp.float32),
                   jax.ShapeDtypeStruct((4, 4, T), jnp.float32)),
        in_specs=[pl.BlockSpec(memory_space=pltpu.HBM)] * 2,
        out_specs=(pl.BlockSpec(memory_space=pltpu.VMEM), pl.BlockSpec(memory_space=pltpu.VMEM)),
        scratch_shapes=scratch + [
            pltpu.VMEM((2, 8, 128), jnp.float32),
            pltpu.VMEM((16, 4 * NA, NB), jnp.float32),
            pltpu.VMEM((2, 4, 4, 8, 128), jnp.float32),
            pltpu.SMEM((8,), jnp.float32), pltpu.SemaphoreType.DMA,
            pltpu.SemaphoreType.DMA((2,)), pltpu.SemaphoreType.DMA((6, 27)),
            pltpu.SemaphoreType.DMA((6, 27)), pltpu.SemaphoreType.DMA((2,)),
            pltpu.SemaphoreType.DMA((2, 4)), pltpu.VMEM((2, 2, 8, 128), jnp.float32)],
        compiler_params=pltpu.CompilerParams(
            collective_id=0, has_side_effects=True, vmem_limit_bytes=48 * 2**20),
        name="moveout",
    )(pltpu.with_memory_space_constraint(offset_weight, pltpu.HBM),
      pltpu.with_memory_space_constraint(data, pltpu.HBM))


def solution(mesh):
    counts = (mesh.shape["il"], mesh.shape["xl"])
    return jax.shard_map(
        lambda data, offset_weight: moveout(data, offset_weight, counts),
        mesh=mesh,
        in_specs=(P("il", "xl", "off", None), P("off")),
        out_specs=(P("il", "xl", "off", None), P("il", "xl", None)),
        check_vma=False,
    )
```

```python
import jax
import jax.numpy as jnp
from jax import lax
from jax.experimental import pallas as pl
from jax.experimental.pallas import tpu as pltpu
from jax.sharding import PartitionSpec as P

T = 1024
NA = 16
NB = 64
damping = 0.05
MESH = pl.DeviceIdType.MESH
STEPS = [(-1, -1), (-1, 1), (1, -1), (1, 1), (0, -1), (0, 1), (0, 0), (-1, 0), (1, 0)]
CENTRE = 9 + STEPS.index((0, 0))
SOURCE = {-1: slice(0, 1), 0: slice(0, 4), 1: slice(3, 4)}
INNER = {-1: slice(1, 2), 0: slice(1, 5), 1: slice(4, 5)}
TARGET = {-1: slice(5, 6), 0: slice(1, 5), 1: slice(0, 1)}
WINDOWS = ((0, 512), (384, 640))
SEAM = 448


def earlier(x, axis):
    x = pltpu.roll(x, 1, axis)
    at = lax.broadcasted_iota(jnp.int32, (8, 128), axis)
    return jnp.concatenate([jnp.where(at == 0, 0.0, x[:, :128]), x[:, 128:]], axis=1)


def later(x, axis):
    n = x.shape[axis]
    x = pltpu.roll(x, n - 1, axis)
    at = lax.broadcasted_iota(jnp.int32, (8, 128), axis)
    return jnp.concatenate([x[:, :n - 128], jnp.where(at == 127, 0.0, x[:, n - 128:])], axis=1)


def smooth_time(u):
    return (earlier(u, 1) + 2.0 * u + later(u, 1)) * (1.0 / 256.0)


def moveout_kernel(counts, weight_hbm, data_hbm, out_ref, stack_ref, *scratch):
    halves, scratch = (scratch[:20], scratch[20:40]), scratch[40:]
    (wsum, raw, part, weight_ref, weight_sem, load_sems, send_sems, recv_sems,
     sum_sems, part_sems, seam_inner) = scratch
    n_il, n_xl = counts
    off, il, xl = lax.axis_index("off"), lax.axis_index("il"), lax.axis_index("xl")
    first = off == 0
    partner = {"off": 1 - off, "il": il, "xl": xl}

    def exists(di, dj):
        i, j = il + di, xl + dj
        return (i >= 0) & (i < n_il) & (j >= 0) & (j < n_xl)

    def transfers(turn, field, planes):
        made = []
        for k, (di, dj) in enumerate(STEPS):
            def copy(slot, to_off, source, target):
                return pltpu.make_async_remote_copy(
                    src_ref=source, dst_ref=target,
                    send_sem=send_sems.at[turn, slot], recv_sem=recv_sems.at[turn, slot],
                    device_id={"off": to_off, "il": il + di, "xl": xl + dj},
                    device_id_type=MESH)
            sends, takes = exists(di, dj), exists(-di, -dj)
            copies = []
            if field is not None and (di, dj) != (0, 0):
                copies.append(copy(k, off, field.at[INNER[di], INNER[dj]],
                                   field.at[TARGET[di], TARGET[dj]]))
            for n, (source, target) in enumerate(planes):
                plane = copy(9 + 9 * n + k, 1 - off, source.at[SOURCE[di], SOURCE[dj]],
                             target.at[TARGET[di], TARGET[dj]])
                if n == 0:
                    copies.append(plane)
                else:
                    made.append((sends & (off == 1), takes & first, [plane], 18 + k))
            if copies:
                made.append((sends, takes, copies, 9 + k))
        return made

    def when_all(made, which, act):
        for item in made:
            @pl.when(item[which])
            def _():
                for copy in item[2]:
                    getattr(copy, act)()

    loads = []
    for n, (base, width) in enumerate(WINDOWS):
        load = pltpu.make_async_copy(
            data_hbm.at[:, :, :, base:base + width], halves[n][0].at[1:5, 1:5], load_sems.at[n])
        load.start()
        loads.append(load)
    load_weight = pltpu.make_async_copy(weight_hbm, weight_ref, weight_sem)
    load_weight.start()
    barrier = pltpu.get_barrier_semaphore()
    for di, dj in STEPS:
        for o in (0, 1):
            if (di, dj, o) != (0, 0, 0):
                @pl.when(exists(di, dj))
                def _():
                    pl.semaphore_signal(
                        barrier, inc=1, device_id_type=MESH,
                        device_id={"off": (off + o) % 2, "il": il + di, "xl": xl + dj})
    rows_near = 1 + (il > 0).astype(jnp.int32) + (il < n_il - 1).astype(jnp.int32)
    cols_near = 1 + (xl > 0).astype(jnp.int32) + (xl < n_xl - 1).astype(jnp.int32)

    load_weight.wait()
    total = weight_ref[0]
    for h in range(1, 8):
        total = total + weight_ref[h]
    wsum[0] = jnp.full((8, 128), total, jnp.float32)
    for load, half in zip(loads, halves):
        load.wait()
        dx, p0, p1 = half[0], half[3], half[4]
        for i in range(4):
            for j in range(4):
                tile = dx[1 + i, 1 + j]
                p0[i, j:j + 1] = jnp.where(first, tile[7:8], tile[0:1])
                p1[i, j:j + 1] = tile[1:2]
    pl.semaphore_wait(barrier, 2 * rows_near * cols_near - 1)

    rounds = []
    for n, half in enumerate(halves):
        dx, d0, d1, p0, p1 = half[:5]
        made = transfers(n, dx, [])
        when_all(made, 0, "start")
        plane = transfers(n, None, [(p0, d0), (p1, d1)])
        when_all(plane, 0, "start")
        rounds.append((made, plane))
    sums = pltpu.make_async_remote_copy(
        src_ref=wsum.at[0], dst_ref=wsum.at[1], send_sem=sum_sems.at[0], recv_sem=sum_sems.at[1],
        device_id=partner, device_id_type=MESH)
    sums.start()

    for di, dj in STEPS:
        if (di, dj) != (0, 0):
            @pl.when(jnp.logical_not(exists(-di, -dj)))
            def _():
                for half in halves:
                    for n in (0, 1, 2, 14, 15, 16, 17):
                        shape = half[n].at[TARGET[di], TARGET[dj]].shape
                        half[n][TARGET[di], TARGET[dj]] = jnp.zeros(shape, jnp.float32)

    keep_next = jnp.where(first, 1.0, 0.0)
    keep_before = 1.0 - keep_next
    row = lax.broadcasted_iota(jnp.int32, (8, 128), 0)
    lane = lax.broadcasted_iota(jnp.int32, (8, 128), 1)

    def smooth_space(field, plane, out):
        def column(c, carry):
            lanes = pl.ds(pl.multiple_of(c * 128, 128), 128)
            sums_xl = []
            for i in range(6):
                tiles = [field[i, j, :, lanes] for j in range(6)]
                pairs = [tiles[j] + tiles[j + 1] for j in range(5)]
                sums_xl.append([pairs[j] + pairs[j + 1] for j in range(4)])
            halo = [plane[i, :, lanes] for i in range(6)]
            for i in range(4):
                h = halo[i] + 2.0 * halo[i + 1] + halo[i + 2]
                h = pltpu.roll(h, 1, 0) + 2.0 * h + pltpu.roll(h, 7, 0)
                before = h * keep_before
                after = h * keep_next
                for j in range(4):
                    x = sums_xl[i][j] + 2.0 * sums_xl[i + 1][j] + sums_xl[i + 2][j]
                    up = jnp.broadcast_to(before[j + 1:j + 2], (8, 128))
                    down = jnp.broadcast_to(after[j + 1:j + 2], (8, 128))
                    up = jnp.where(row == 0, up, pltpu.roll(x, 1, 0))
                    down = jnp.where(row == 7, down, pltpu.roll(x, 7, 0))
                    out[i, j, :, lanes] = up + 2.0 * x + down
            return carry
        lax.fori_loop(0, field.shape[3] // 128, column, 0, unroll=True)

    def smooth_inner(field, out):
        def column(c, carry):
            lanes = pl.ds(pl.multiple_of(c * 128, 128), 128)
            sums_xl = []
            for i in range(1, 5):
                tiles = [field[i, j, :, lanes] for j in range(1, 5)]
                pairs = [tiles[j] + tiles[j + 1] for j in range(3)]
                sums_xl.append([pairs[j] + pairs[j + 1] for j in range(2)])
            for i in range(2):
                for j in range(2):
                    x = sums_xl[i][j] + 2.0 * sums_xl[i + 1][j] + sums_xl[i + 2][j]
                    up = jnp.where(row == 0, 0.0, pltpu.roll(x, 1, 0))
                    down = jnp.where(row == 7, 0.0, pltpu.roll(x, 7, 0))
                    out[1 + i, 1 + j, :, lanes] = up + 2.0 * x + down
            return carry
        lax.fori_loop(0, field.shape[3] // 128, column, 0, unroll=True)

    def first_turn(n, inner):
        dx, d0, d1, _, _, gg, gr, hgg, hgr, grad, res, rden, ub, uc, q2, o2, q3, o3, pq, own = \
            halves[n]
        width = WINDOWS[n][1]
        row8 = lax.broadcasted_iota(jnp.int32, (8, width), 0)

        def gradients(i, j):
            d = dx[i, j]
            edge = jnp.broadcast_to(d0[i, j:j + 1] * keep_next, (8, width))
            f = jnp.where(row8 == 7, edge, pltpu.roll(d, 7, 0))
            r = f - d
            s = d + f
            g = 0.25 * (later(s, 1) - earlier(s, 1))
            gg[i, j] = g * g
            gr[i, j] = g * r
            grad[i, j] = g
            res[i, j] = r

        made, plane = rounds[n]
        if inner:
            centre = [item for item in plane if item[3] == CENTRE]
            when_all(centre, 1, "wait_recv")
            for i in range(1, 5):
                for j in range(1, 5):
                    gradients(i, j)
            return
        when_all(made + [item for item in plane if item[3] != CENTRE], 1, "wait_recv")

        @pl.when(off == 1)
        def _():
            for i in range(6):
                for j in range(6):
                    d1[i, j:j + 1] = dx[i, j, 0:1]

        for i in range(6):
            for j in range(6):
                if i in (0, 5) or j in (0, 5):
                    gradients(i, j)
            d, f = d0[i], d1[i]
            s = d + f
            g = 0.25 * (later(s, 1) - earlier(s, 1))
            hgg[i] = g * g
            hgr[i] = g * (f - d)

        smooth_space(gg, hgg, ub)
        smooth_space(gr, hgr, uc)

        def start_slope(i, carry):
            for j in range(4):
                inverse = 1.0 / (smooth_time(ub[i, j]) + damping)
                rden[i, j] = inverse
                slope = -smooth_time(uc[i, j]) * inverse
                own[i, j] = slope
                g = grad[i + 1, j + 1]
                q = g * (res[i + 1, j + 1] + slope * g)
                q2[i + 1, j + 1] = q
                pq[0, i, j:j + 1] = jnp.where(first, q[7:8], q[0:1])
            return carry

        lax.fori_loop(0, 4, start_slope, 0, unroll=True)
        made = transfers(2 + n, q2, [(pq.at[0], o2)])
        when_all(made, 0, "start")
        rounds.append(made)

    def second_turn(n):
        grad, res, rden, ub, q2, o2, q3, pq, own = (halves[n][k] for k in (
            9, 10, 11, 12, 14, 15, 16, 18, 19))
        smooth_space(q2, o2, ub)

        def next_slope(i, carry):
            for j in range(4):
                slope = own[i, j] - smooth_time(ub[i, j]) * rden[i, j]
                own[i, j] = slope
                g = grad[i + 1, j + 1]
                q = g * (res[i + 1, j + 1] + slope * g)
                q3[i + 1, j + 1] = q
                pq[1, i, j:j + 1] = jnp.where(first, q[7:8], q[0:1])
            return carry

        lax.fori_loop(0, 4, next_slope, 0, unroll=4)
        made = transfers(4 + n, q3, [(pq.at[1], halves[n][17])])
        when_all(made, 0, "start")
        rounds.append(made)

    weight = jnp.full((8, 128), weight_ref[0], jnp.float32)
    for h in range(1, 8):
        weight = jnp.where(row == h, weight_ref[h], weight)
    edge_row = jnp.where(first, 7, 0)
    inner_weight = jnp.where(row == edge_row, 0.0, weight)
    high = lax.broadcasted_iota(jnp.int32, (NA, 128), 0)
    high = jnp.where(high < 8, 2 * high, 2 * high - 15)
    high = high.astype(jnp.float32).astype(jnp.bfloat16)
    low = lax.broadcasted_iota(jnp.int32, (NB, 128), 0).astype(jnp.float32).astype(jnp.bfloat16)
    zero_a = jnp.zeros((NA, 128), jnp.bfloat16)
    zero_b = jnp.zeros((NB, 128), jnp.bfloat16)
    one_b = jnp.ones((NB, 128), jnp.bfloat16)

    def push(data, slope, start, kind="full"):
        width = data.shape[1]
        tt = lax.broadcasted_iota(jnp.int32, (8, width), 1).astype(jnp.float32) + (start + 1.0)
        hh = lax.broadcasted_iota(jnp.int32, (8, width), 0).astype(jnp.float32) + 0.5
        hh = hh + 8.0 * keep_before
        place = jnp.sqrt(jnp.maximum(tt * tt - tt * hh * slope, 1.0)) - 1.0
        cell = jnp.floor(place)
        f = place - cell
        cell = jnp.minimum(cell, float(T))
        a = jnp.floor(cell * (1.0 / NB))
        b = cell - a * NB
        scale = inner_weight if kind == "inner" else weight
        v = data * jnp.concatenate([scale] * (width // 128), axis=1)
        x1 = v * f
        x0 = v - x1
        x0h = x0.astype(jnp.bfloat16).astype(jnp.float32)
        x1h = x1.astype(jnp.bfloat16).astype(jnp.float32)
        values = (x0h, x0 - x0h, x1h, x1 - x1h)
        groups = [(h, h + 1) for h in range(0, 8, 2)]
        if kind == "edge":
            a, b, *values = [jnp.where(first, x[7:8], x[0:1]) for x in (a, b) + values]
            groups = [(0,)]
        acc = jnp.zeros((4 * NA, NB), jnp.float32)
        for group in groups:
            left, right = [], []
            for k in group:
                for c in range(0, width, 128):
                    def spread(x, n):
                        piece = x[k:k + 1, c:c + 128]
                        return jnp.broadcast_to(piece, (n, 128)).astype(jnp.bfloat16)
                    hit = spread(a, NA) == high
                    left.append(jnp.concatenate(
                        [jnp.where(hit, spread(x, NA), zero_a) for x in values], axis=0))
                    right.append(jnp.where(spread(b, NB) == low, one_b, zero_b))
            dot = lax.dot_general(
                jnp.concatenate(left, axis=1), jnp.concatenate(right, axis=1),
                (((1,), (1,)), ((), ())), preferred_element_type=jnp.float32)
            acc = acc + jnp.maximum(dot, -3.0e38)
        return acc

    def gather(i):
        for j in range(4):
            acc = raw[4 * i + j]
            lower = acc[:NA] + acc[NA:2 * NA]
            upper = acc[2 * NA:3 * NA] + acc[3 * NA:]
            lower = jnp.concatenate([lower[:8], lower[8:]], axis=1)
            upper = jnp.concatenate([upper[:8], upper[8:]], axis=1)
            upper = pltpu.roll(upper, 1, 1)
            before = pltpu.roll(upper, 1, 0)
            upper = jnp.where(lane == 0, jnp.where(row == 0, 0.0, before), upper)
            part[0, i, j] = lower + upper

    def exchange(i):
        return pltpu.make_async_remote_copy(
            src_ref=part.at[0, i], dst_ref=part.at[1, i],
            send_sem=part_sems.at[0, i], recv_sem=part_sems.at[1, i],
            device_id=partner, device_id_type=MESH)

    def last_slope(n, i, j):
        rden, ub, own = (halves[n][k] for k in (11, 12, 19))
        return own[i, j] - smooth_time(ub[i, j]) * rden[i, j]

    def push_first(i, j, kind):
        slope = last_slope(0, i, j)
        added = push(halves[0][0][i + 1, j + 1, :, :384], slope[:, :384], 0.0, kind)
        if kind == "inner":
            seam_inner[i - 1, j - 1] = slope[:, 384:]
        else:
            halves[0][19][i, j] = slope
            out_ref[i, j, :, :384] = slope[:, :384]
        if kind == "edge":
            added = raw[4 * i + j] + added
        raw[4 * i + j] = added

    def push_second(i, j, kind):
        slope = last_slope(1, i, j)
        before = seam_inner[i - 1, j - 1] if kind == "inner" else halves[0][19][i, j, :, 384:]
        seam = jnp.where(lane < SEAM - 384, before, slope[:, :128])
        slope = jnp.concatenate([seam, slope[:, 128:]], axis=1)
        if kind != "inner":
            out_ref[i, j, :, 384:] = slope
        added = push(halves[1][0][i + 1, j + 1], slope, 384.0, kind)
        raw[4 * i + j] = raw[4 * i + j] + added

    inner = [(i, j) for i in (1, 2) for j in (1, 2)]
    sides = [(i, j) for i in (1, 2) for j in (0, 3)]

    for n in (0, 1):
        first_turn(n, True)
        first_turn(n, False)
    for made in rounds[0] + rounds[1]:
        when_all(made, 0, "wait_send")
    for n in (0, 1):
        when_all(rounds[2 + n], 1, "wait_recv")
        second_turn(n)
    smooth_inner(halves[0][16], halves[0][12])
    for i, j in inner:
        push_first(i, j, "inner")
    smooth_inner(halves[1][16], halves[1][12])
    for i, j in inner:
        push_second(i, j, "inner")
    for made in rounds[2:4]:
        when_all(made, 0, "wait_send")

    when_all(rounds[4], 1, "wait_recv")
    smooth_space(halves[0][16], halves[0][17], halves[0][12])

    def push_row(k, carry):
        for j in range(4):
            push_first(3 * k, j, "full")
        return carry

    lax.fori_loop(0, 2, push_row, 0)
    for i, j in sides:
        push_first(i, j, "full")
    for i, j in inner:
        push_first(i, j, "edge")
    when_all(rounds[4], 0, "wait_send")
    when_all(rounds[5], 1, "wait_recv")
    smooth_space(halves[1][16], halves[1][17], halves[1][12])
    for j in range(4):
        push_second(0, j, "full")
    gather(0)
    for i, j in sides:
        push_second(i, j, "full")
    for i, j in inner:
        push_second(i, j, "edge")
    exchange(0).start()
    gather(1)
    gather(2)
    for j in range(4):
        push_second(3, j, "full")
    exchange(1).start()
    exchange(2).start()
    gather(3)
    exchange(3).start()
    when_all(rounds[5], 0, "wait_send")
    sums.wait_recv()
    weights = wsum[0] + wsum[1]
    for i in range(4):
        exchange(i).wait_recv()
        for j in range(4):
            stacked = (part[0, i, j] + part[1, i, j]) / weights
            for r in range(8):
                stack_ref[i, j:j + 1, 128 * r:128 * r + 128] = stacked[r:r + 1]
    sums.wait_send()
    for i in range(4):
        exchange(i).wait_send()


def moveout(data, offset_weight, counts):
    scratch = []
    for _, width in WINDOWS:
        tiles = pltpu.VMEM((6, 6, 8, width), jnp.float32)
        plane = pltpu.VMEM((6, 8, width), jnp.float32)
        own = pltpu.VMEM((4, 4, 8, width), jnp.float32)
        rows = pltpu.VMEM((4, 8, width), jnp.float32)
        scratch += [tiles, plane, plane, rows, rows, tiles, tiles, plane, plane, tiles, tiles,
                    own, own, own, tiles, plane, tiles, plane,
                    pltpu.VMEM((2, 4, 8, width), jnp.float32), own]
    return pl.pallas_call(
        lambda *refs: moveout_kernel(counts, *refs),
        out_shape=(jax.ShapeDtypeStruct((4, 4, 8, T), jnp.float32),
                   jax.ShapeDtypeStruct((4, 4, T), jnp.float32)),
        in_specs=[pl.BlockSpec(memory_space=pltpu.HBM)] * 2,
        out_specs=(pl.BlockSpec(memory_space=pltpu.VMEM), pl.BlockSpec(memory_space=pltpu.VMEM)),
        scratch_shapes=scratch + [
            pltpu.VMEM((2, 8, 128), jnp.float32),
            pltpu.VMEM((16, 4 * NA, NB), jnp.float32),
            pltpu.VMEM((2, 4, 4, 8, 128), jnp.float32),
            pltpu.SMEM((8,), jnp.float32), pltpu.SemaphoreType.DMA,
            pltpu.SemaphoreType.DMA((2,)), pltpu.SemaphoreType.DMA((6, 27)),
            pltpu.SemaphoreType.DMA((6, 27)), pltpu.SemaphoreType.DMA((2,)),
            pltpu.SemaphoreType.DMA((2, 4)), pltpu.VMEM((2, 2, 8, 128), jnp.float32)],
        compiler_params=pltpu.CompilerParams(
            collective_id=0, has_side_effects=True, vmem_limit_bytes=48 * 2**20),
        name="moveout",
    )(pltpu.with_memory_space_constraint(offset_weight, pltpu.HBM),
      pltpu.with_memory_space_constraint(data, pltpu.HBM))


def solution(mesh):
    counts = (mesh.shape["il"], mesh.shape["xl"])
    return jax.shard_map(
        lambda data, offset_weight: moveout(data, offset_weight, counts),
        mesh=mesh,
        in_specs=(P("il", "xl", "off", None), P("off")),
        out_specs=(P("il", "xl", "off", None), P("il", "xl", None)),
        check_vma=False,
    )
```
